512 devices in a mesh: ctx: 64 (over y, z_hi, x, core), tp: 8 (over z_lo).
Axes of the slice: x: 4, y: 4, z: 16 (z_hi: 2, z_lo: 8; z = z_hi * 8 + z_lo), core: 2. Of those that a mesh axis runs over, the one named last changes fastest.
Arguments:
- hyena_in: bfloat16 [16384, 3, 4096], P('ctx', None, 'tp'), may hold values from -6 to 6
- filters: float32 [128, 4096], P(None, 'tp'), may hold values from -0.5 to 0.5
- attn_in: bfloat16 [16384, 3, 4096], P('ctx', None, 'tp'), may hold values from -18.5 to 18.5
- out_weight: bfloat16 [4096, 4096], P('tp', 'ctx'), may hold values from -0.25 to 0.25
- attn_weight: bfloat16 [4096, 4096], P('tp', 'ctx'), may hold values from -0.25 to 0.25
Outputs:
- block_out: bfloat16 [16384, 4096], P('ctx', 'tp')
- attn_block: bfloat16 [16384, 4096], P('ctx', 'tp')
The draws below stay inside these ranges and needn't reach their ends.
All inputs are finite; a program needn't handle non-finite values.
Results may differ from the reference program's by a relative error of at most 0.014.
Values may be sent and summed in bfloat16 or wider, within the bound.
A program may use at most 64 MiB of HBM per device.

```python
import math
import jax
import jax.numpy as jnp
from jax import lax

D = 4096
HEADS = 32
HEAD_DIM = 128
TAPS = 128
WINDOW = 2048
CHANNELS = 4096
TOKENS = 16384
N_TP = 8


def draw_attn_in(key, part):
    key_query, key_keys, key_values = jax.random.split(jax.random.fold_in(key, 7), 3)
    shape = (TOKENS, CHANNELS)
    queries = jnp.clip(jax.random.normal(key_query, shape, jnp.float32), -4.0, 4.0)
    keys_drawn = 3.0 * jnp.clip(jax.random.normal(key_keys, shape, jnp.float32), -4.0, 4.0)
    values = jnp.clip(jax.random.normal(key_values, shape, jnp.float32), -4.0, 4.0)
    return jnp.stack([queries, keys_drawn, values], 1).astype(jnp.bfloat16)


def with_spikes(values, rng, source, target, parts, factor):
    def block_of(dim):
        return (jnp.arange(values.shape[dim]) // (values.shape[dim] // parts)).reshape((-1,) + (1,) * (values.ndim - 1 - dim))

    first = jax.random.permutation(rng, parts)[block_of(target)]
    second = (block_of(target) + parts // 2) % parts
    return jnp.where((block_of(source) == first) | (block_of(source) == second), factor * values, values)


def shard_levels(stream_key, dims, cuts, smallest, largest):
    factor_of, own = 1.0, jax.random.fold_in(stream_key, 6)
    for dim, blocks in cuts:
        draws = jnp.exp(jax.random.uniform(jax.random.fold_in(own, dim), (blocks,), jnp.float32, smallest / len(cuts), largest / len(cuts)))
        factor_of = factor_of * jnp.repeat(draws, dims[dim] // blocks).reshape([-1 if axis == dim else 1 for axis in range(len(dims))])
    return factor_of


def normal_values(key, dims, spread, most, cuts=(), held_as=jnp.bfloat16):
    factor_of = shard_levels(key, dims, cuts, -0.22, 0.18) if cuts else 1.0
    entries = jax.random.normal(key, dims, jnp.float32) * spread * factor_of
    return jnp.minimum(jnp.maximum(entries, -most), most).astype(held_as)


def heavy_noise(rng, dims, spread, bound, cuts, heavy, held_as=jnp.bfloat16):
    values = spread * jax.random.normal(rng, dims, jnp.float32)
    if cuts:
        values = values * shard_levels(rng, dims, cuts, -0.22, 0.18)
    return jnp.clip(with_spikes(values, jax.random.fold_in(rng, 3), *heavy), -bound, bound).astype(held_as)


def setup_inputs(seed: int = 0) -> dict:
    splits = jax.random.split(jax.random.key(seed), 6)
    return {
        "hyena_in": normal_values(splits[0], (TOKENS, 3, CHANNELS), 1.0, 6.0, ((0, 64), (2, 8))),
        "filters": normal_values(splits[1], (TAPS, CHANNELS), TAPS ** -0.5, 0.5, ((1, 8),), jnp.float32),
        "attn_in": draw_attn_in(jax.random.fold_in(splits[5], 71), 0),
        "out_weight": heavy_noise(splits[3], (CHANNELS, D), CHANNELS ** -0.5, 0.25, ((0, 8), (1, 64)), (0, 1, 64, 4.0)),
        "attn_weight": heavy_noise(splits[4], (CHANNELS, D), CHANNELS ** -0.5, 0.25, ((0, 8), (1, 64)), (0, 1, 64, 4.0)),
    }


def depthwise(padded, filters):
    taps = filters.shape[0]
    length = padded.shape[0] - taps + 1

    def add_tap(index, total):
        window_rows = lax.dynamic_slice_in_dim(padded, (taps - 1 - index).astype(jnp.int32), length, 0)
        return total + filters[index][None, :] * window_rows
    return lax.fori_loop(0, taps, add_tap, jnp.zeros((length, padded.shape[1]), jnp.float32))

def head_attention(queries, keys_all, values_all, first_query, first_key):
    scores = lax.dot_general(queries, keys_all, (((1,), (1,)), ((), ())), preferred_element_type=jnp.float32)
    scores = scores * (1.0 / math.sqrt(HEAD_DIM))
    query_pos = first_query + lax.iota(jnp.int32, queries.shape[0])
    key_pos = first_key + lax.iota(jnp.int32, keys_all.shape[0])
    valid = (key_pos[None, :] <= query_pos[:, None]) & (key_pos[None, :] > query_pos[:, None] - WINDOW) & (key_pos[None, :] >= 0)
    scores = jnp.where(valid, scores, -jnp.inf)
    top = lax.optimization_barrier(jnp.max(scores, axis=1, keepdims=True))
    weights = jnp.exp(scores - top)
    total = lax.optimization_barrier(jnp.sum(weights, axis=1, keepdims=True))
    probs = weights.astype(jnp.bfloat16)
    return jnp.dot(probs, values_all, preferred_element_type=jnp.float32) / total

def split_heads(array):
    return array.reshape(array.shape[0], HEADS, HEAD_DIM).transpose(1, 0, 2)

def project_groups(acts, weight):
    width = CHANNELS // N_TP
    summed = jnp.zeros((TOKENS, D), jnp.float32)
    for group in range(N_TP):
        term = jnp.dot(acts[:, group * width:(group + 1) * width], weight[group * width:(group + 1) * width], preferred_element_type=jnp.float32).astype(jnp.bfloat16)
        term = lax.optimization_barrier(term)
        summed = summed + term.astype(jnp.float32)
    return summed.astype(jnp.bfloat16)

def reference(hyena_in, filters, attn_in, out_weight, attn_weight):
    product = (hyena_in[:, 0].astype(jnp.float32) * hyena_in[:, 2].astype(jnp.float32)).astype(jnp.bfloat16)
    padded = jnp.concatenate([jnp.zeros((TAPS - 1, CHANNELS), jnp.float32), product.astype(jnp.float32)], 0)
    filtered = depthwise(padded, filters)
    hyena_act = (hyena_in[:, 1].astype(jnp.float32) * filtered).astype(jnp.bfloat16)
    block = math.gcd(TOKENS, 512)
    padding = jnp.zeros((WINDOW, CHANNELS), jnp.bfloat16)
    query_heads = split_heads(attn_in[:, 0])
    key_heads = split_heads(jnp.concatenate([padding, attn_in[:, 1]], 0))
    value_heads = split_heads(jnp.concatenate([padding, attn_in[:, 2]], 0))
    starts = jnp.arange(TOKENS // block, dtype=jnp.int32) * block

    def one_head(operands):
        query_one, key_one, value_one = operands

        def one_block(start):
            query_block = lax.dynamic_slice_in_dim(query_one, start, block, 0)
            key_block = lax.dynamic_slice_in_dim(key_one, start, block + WINDOW, 0)
            value_block = lax.dynamic_slice_in_dim(value_one, start, block + WINDOW, 0)
            return head_attention(query_block, key_block, value_block, start, start - WINDOW)
        return lax.map(one_block, starts).reshape(TOKENS, HEAD_DIM)
    attended = lax.map(one_head, (query_heads, key_heads, value_heads))
    attended = attended.transpose(1, 0, 2).reshape(TOKENS, CHANNELS).astype(jnp.bfloat16)
    return (project_groups(hyena_act, out_weight), project_groups(attended, attn_weight))
```

```python
import functools
import math

import jax
import jax.numpy as jnp
from jax import lax
from jax.experimental import pallas as pl
from jax.experimental.pallas import tpu as pltpu
from jax.sharding import PartitionSpec as P

HEAD_DIM = 128
WINDOW = 2048
GROUPS = 2
F32 = jnp.float32
BF16 = jnp.bfloat16


def kernel(
    window,
    hyena,
    filters,
    attn,
    w_hyena,
    w_attn,
    out_h,
    out_a,
    kv,
    wg,
    part,
    from_left,
    from_right,
    rim,
    padded,
    shifted,
    act,
    scores,
    kv_recv,
    kv_send,
    w_recv,
    w_send,
    rs_recv,
    rs_send,
    rim_recv,
    rim_send,
):
    _, rows, width = attn.shape
    heads = width // HEAD_DIM
    taps = filters.shape[0]
    n_ctx = lax.axis_size("ctx")
    n_tp = lax.axis_size("tp")
    slots = window // rows
    n_x = slots // 2
    n_y = n_ctx // (2 * slots)
    piece = w_hyena.shape[0]
    pair = 2 * piece
    row_w = slots * piece
    dest_w = out_h.shape[1]
    half = rows // GROUPS

    me = lax.axis_index("ctx")
    t = lax.axis_index("tp")
    row = me // slots
    i = me % slots
    y = row // 2
    zh = row % 2
    x = i // 2
    k = i % 2
    n_rows = n_ctx // slots

    def at(y_, zh_, x_, k_):
        return ((y_ * 2 + zh_) * n_x + x_) * 2 + k_

    partner = at(y, zh, x, 1 - k)
    flip = at(y, 1 - zh, x, k)
    row_next = lax.rem(row + 1, n_rows) * slots + i
    row_prev = lax.rem(row + n_rows - 1, n_rows) * slots + i
    after = lax.rem(me + 1, n_ctx)
    before = lax.rem(me + n_ctx - 1, n_ctx)
    x_peer = [at(y, zh, lax.rem(x + d, n_x), k) for d in range(1, n_x)]
    y_peer = [at(lax.rem(y + d, n_y), zh, x, k) for d in range(1, n_y)]

    barrier = pltpu.get_barrier_semaphore()
    peers = [partner, flip, row_next, row_prev, after, before] + x_peer + y_peer
    for peer in peers:
        pl.semaphore_signal(barrier, inc=1, device_id={"ctx": peer})

    @pl.when(t > 0)
    def _():
        pl.semaphore_signal(barrier, inc=1, device_id={"tp": t - 1})

    @pl.when(t < n_tp - 1)
    def _():
        pl.semaphore_signal(barrier, inc=1, device_id={"tp": t + 1})

    beside = (t > 0).astype(jnp.int32) + (t < n_tp - 1).astype(jnp.int32)
    pl.semaphore_wait(barrier, len(peers) + beside)

    def remote(src, dst, send, recv, peer, axis="ctx"):
        return pltpu.make_async_remote_copy(
            src_ref=src, dst_ref=dst, send_sem=send, recv_sem=recv, device_id={axis: peer}
        )

    def lanes(h):
        return pl.ds(pl.multiple_of(h * HEAD_DIM, HEAD_DIM), HEAD_DIM)

    def own_kv(h):
        return attn.at[pl.ds(1, 2), :, lanes(h)]

    def slot_kv(j, h):
        return kv.at[:, j, :, lanes(h)]

    def kv_copy(src, h, j, n, peer):
        return remote(src, slot_kv(j, h), kv_send.at[h, n], kv_recv.at[h, j], peer)

    def flip_kv(h):
        return kv_copy(own_kv(h), h, i, 0, row_next)

    def along(h, d, src):
        return kv_copy(src, h, i, d, x_peer[d - 1])

    def to_partner(h, src):
        return kv_copy(src, h, i, n_x, partner)

    def came(d):
        return lax.rem(x + d, n_x) * 2 + k

    def forward(h, d):
        j = came(d)
        return kv_copy(slot_kv(j, h), h, j, n_x + d, partner)

    def start_own(h):
        for d in range(1, n_x):

            @pl.when(x + d < n_x)
            def _():
                along(h, d, own_kv(h)).start()

        @pl.when(k == 0)
        def _():
            to_partner(h, own_kv(h)).start()

    def arrived(h, j):
        pltpu.make_async_copy(slot_kv(j, h), slot_kv(j, h), kv_recv.at[h, j]).wait()

    def spread(h):
        arrived(h, i)
        for d in range(1, n_x):

            @pl.when(x + d >= n_x)
            def _():
                along(h, d, slot_kv(i, h)).start()

        @pl.when(k == 1)
        def _():
            to_partner(h, slot_kv(i, h)).start()

    def pass_on(h):
        for d in range(1, n_x):
            arrived(h, came(d))
            forward(h, d).start()

    def rest(h):
        for d in range(n_x):
            arrived(h, lax.rem(x + d, n_x) * 2 + 1 - k)

    def w_rows(first, count):
        return pl.ds(pl.multiple_of(first * piece, piece), count * piece)

    def w_block(layer, first, count):
        return wg.at[layer, w_rows(first, count)]

    def w_copy(block, n, peer):
        return remote(block, block, w_send.at[n], w_recv.at[n], peer)

    def w_swap(src):
        return remote(src, w_block(1 - k, me, 1), w_send.at[0], w_recv.at[0], partner)

    def w_landed(block, n):
        pltpu.make_async_copy(block, block, w_recv.at[n]).wait()

    chip = me - k
    chip_flip = flip - k

    def w_own(ref):
        return pltpu.make_async_copy(ref, w_block(k, me, 1), w_recv.at[1])

    def w_flip():
        return w_copy(w_block(k, chip, 2), 2, flip)

    def w_along(d, other):
        return w_copy(
            w_block(k, chip_flip if other else chip, 2), 2 + d + (n_x - 1) * other, x_peer[d - 1]
        )

    base_y = 2 + 2 * n_x - 1

    def w_up(d):
        return w_copy(w_block(k, y * 2 * slots, 2 * slots), base_y + d, y_peer[d - 1])

    base_p = base_y + n_y

    def w_hand(d):
        y_ = lax.rem(y + d, n_y)
        block = w_block(k, y_ * 2 * slots, 2 * slots)
        return w_copy(block, base_p + d, partner)

    flip_kv(0).start()
    rim_rows = pl.ds(rows - taps, taps)
    for n in range(2):
        remote(hyena.at[2 * n, rim_rows], rim.at[n], rim_send.at[n], rim_recv.at[n], after).start()

    @pl.when(k == 0)
    def _():
        w_swap(w_attn).start()
        w_own(w_hyena).start()

    @pl.when(k == 1)
    def _():
        w_swap(w_hyena).start()
        w_own(w_attn).start()

    start_own(0)
    w_landed(w_block(k, me, 1), 1)
    w_landed(w_block(k, partner, 1), 0)
    w_flip().start()
    for d in range(1, n_x):
        w_along(d, 0).start()

    @pl.loop(1, heads)
    def _(h):
        flip_kv(h).start()
        start_own(h)

    own = (hyena[0].astype(F32) * hyena[2].astype(F32)).astype(BF16).astype(F32)
    padded[pl.ds(taps, rows), :] = own
    for n in range(2):
        pltpu.make_async_copy(rim.at[n], rim.at[n], rim_recv.at[n]).wait()
    rim_product = (rim[0].astype(F32) * rim[1].astype(F32)).astype(BF16).astype(F32)
    padded[pl.ds(0, taps), :] = jnp.where(me > 0, rim_product, 0.0)

    total_rows = taps + rows

    @pl.loop(0, width // 128)
    def _(tile):
        cols = pl.ds(pl.multiple_of(tile * 128, 128), 128)
        for s in range(8):
            shifted[s, pl.ds(8, total_rows - 8), :] = padded[pl.ds(8 - s, total_rows - 8), cols]

        chunk = min(rows, 128)

        @pl.loop(0, rows // chunk)
        def _(part_row):
            first = part_row * chunk

            def eight(a, acc):
                coef = filters[pl.ds(pl.multiple_of(a * 8, 8), 8), cols]
                start = pl.multiple_of(taps + first - a * 8, 8)
                for s in range(8):
                    acc = acc + coef[s : s + 1, :] * shifted[s, pl.ds(start, chunk), :]
                return acc

            acc = lax.fori_loop(0, taps // 8, eight, jnp.zeros((chunk, 128), F32))
            at_rows = pl.ds(pl.multiple_of(first, chunk), chunk)
            act[at_rows, cols] = (hyena[1, at_rows, cols].astype(F32) * acc).astype(BF16)

    w_landed(w_block(k, chip_flip, 2), 2)
    for d in range(1, n_x):
        w_along(d, 1).start()
    spread(0)
    for d in range(1, n_x):
        x_ = lax.rem(x + n_x - d, n_x)
        w_landed(w_block(k, at(y, zh, x_, 0), 2), 2 + d)
    for d in range(1, n_x):
        x_ = lax.rem(x + n_x - d, n_x)
        w_landed(w_block(k, at(y, 1 - zh, x_, 0), 2), 2 + d + n_x - 1)
    for d in range(1, n_y):
        w_up(d).start()
    w_hand(0).start()
    pass_on(0)

    @pl.loop(1, heads)
    def _(h):
        spread(h)
        pass_on(h)

    for d in range(1, n_y):
        y_ = lax.rem(y + n_y - d, n_y)
        w_landed(w_block(k, y_ * 2 * slots, 2 * slots), base_y + d)
        w_hand(n_y - d).start()
    for d in range(n_y):
        y_ = lax.rem(y + d, n_y)
        w_landed(w_block(1 - k, y_ * 2 * slots, 2 * slots), base_p + d)

    def project(layer):
        @pl.loop(0, n_tp)
        def _(d):
            weight = wg[layer, pl.ds(pl.multiple_of(d * dest_w, dest_w), dest_w), :]
            part[layer, d] = lax.dot_general(
                act[...], weight, (((1,), (1,)), ((), ())), preferred_element_type=F32
            ).astype(BF16)

    def rs_copy(layer, way, d, g):
        piece_of = (d, pl.ds(pl.multiple_of(g * half, half), half))
        buffer = (from_left, from_right)[way]
        return remote(
            part.at[(layer,) + piece_of],
            buffer.at[(layer,) + piece_of],
            rs_send.at[layer, way, d, g],
            rs_recv.at[layer, way, d, g],
            (t + 1, t - 1)[way],
            "tp",
        )

    def rs_add(layer, way, d, g):
        piece_of = (layer, d, pl.ds(pl.multiple_of(g * half, half), half))
        buffer = (from_left, from_right)[way]
        landed = buffer.at[piece_of]
        pltpu.make_async_copy(landed, landed, rs_recv.at[layer, way, d, g]).wait()
        part[piece_of] = (part[piece_of].astype(F32) + buffer[piece_of].astype(F32)).astype(BF16)

    def rs_step(layer, step):
        m = step // GROUPS
        g = step % GROUPS
        right = n_tp - 1 - m
        left = m

        @pl.when((t < right) & (t > 0))
        def _():
            rs_add(layer, 0, right, g)

        @pl.when(t < right)
        def _():
            rs_copy(layer, 0, right, g).start()

        @pl.when((t > left) & (t < n_tp - 1))
        def _():
            rs_add(layer, 1, left, g)

        @pl.when(t > left)
        def _():
            rs_copy(layer, 1, left, g).start()

    rs_steps = (n_tp - 1) * GROUPS

    def finish(layer, out):
        total = part[layer, t].astype(F32)
        for way in range(2):

            @pl.when((t > 0) if way == 0 else (t < n_tp - 1))
            def _():
                for g in range(GROUPS):
                    buffer = (from_left, from_right)[way]
                    landed = buffer.at[layer, t, pl.ds(g * half, half)]
                    pltpu.make_async_copy(landed, landed, rs_recv.at[layer, way, t, g]).wait()

        left = jnp.where(t > 0, from_left[layer, t].astype(F32), 0.0)
        right = jnp.where(t < n_tp - 1, from_right[layer, t].astype(F32), 0.0)
        out[...] = (total + left + right).astype(BF16)

    project(0)

    scale = 1.0 / math.sqrt(HEAD_DIM)
    gap = lax.broadcasted_iota(jnp.int32, (rows, rows), 1) - lax.broadcasted_iota(
        jnp.int32, (rows, rows), 0
    )

    def attend(h):
        queries = attn[0, :, lanes(h)]

        def block_scores(keys):
            return (
                lax.dot_general(
                    queries, keys, (((1,), (1,)), ((), ())), preferred_element_type=F32
                )
                * scale
            )

        def fold(op, block):
            kept = block[:, :128]
            for n in range(1, rows // 128):
                kept = op(kept, block[:, n * 128 : (n + 1) * 128])
            return kept

        own = jnp.where(gap <= 0, block_scores(attn[1, :, lanes(h)]), -jnp.inf)
        scores[:, slots * rows :] = own
        top = fold(jnp.maximum, own)
        for j in range(slots):
            least = jnp.where(i == j, 0, -rows)
            least = jnp.where((row == 0) & (i <= j), rows, least)
            block = jnp.where(gap > least, block_scores(kv[0, j, :, lanes(h)]), -jnp.inf)
            scores[:, j * rows : (j + 1) * rows] = block
            top = jnp.maximum(top, fold(jnp.maximum, block))
        top = jnp.max(top, axis=1, keepdims=True)
        total = jnp.zeros((rows, 128), F32)
        result = jnp.zeros((rows, HEAD_DIM), F32)
        for j in range(slots + 1):
            weights = jnp.exp(scores[:, j * rows : (j + 1) * rows] - top)
            total = total + fold(jnp.add, weights)
            values = attn[2, :, lanes(h)] if j == slots else kv[1, j, :, lanes(h)]
            result = result + jnp.dot(weights.astype(BF16), values, preferred_element_type=F32)
        total = jnp.sum(total, axis=1, keepdims=True)
        act[:, lanes(h)] = (result / total).astype(BF16)

    per_head = -(-rs_steps // heads)

    @pl.loop(0, heads)
    def _(h):
        rest(h)
        attend(h)

        @pl.loop(h * per_head, jnp.minimum((h + 1) * per_head, rs_steps))
        def _(step):
            rs_step(0, step)

    project(1)

    @pl.loop(0, rs_steps)
    def _(step):
        rs_step(1, step)

    finish(0, out_h)
    finish(1, out_a)

    for n in range(2):
        remote(hyena.at[2 * n, rim_rows], rim.at[n], rim_send.at[n], rim_recv.at[n], after).wait_send()
    w_swap(w_attn).wait_send()
    w_flip().wait_send()
    for d in range(1, n_x):
        w_along(d, 0).wait_send()
        w_along(d, 1).wait_send()
    for d in range(1, n_y):
        w_up(d).wait_send()
    for d in range(n_y):
        w_hand(d).wait_send()

    @pl.loop(0, heads)
    def _(h):
        flip_kv(h).wait_send()
        for d in range(1, n_x):
            along(h, d, own_kv(h)).wait_send()
            forward(h, d).wait_send()
        to_partner(h, own_kv(h)).wait_send()

    @pl.loop(0, rs_steps)
    def _(step):
        m = step // GROUPS
        g = step % GROUPS
        for layer in range(2):

            @pl.when(t < n_tp - 1 - m)
            def _():
                rs_copy(layer, 0, n_tp - 1 - m, g).wait_send()

            @pl.when(t > m)
            def _():
                rs_copy(layer, 1, m, g).wait_send()


def per_device(window, n_tp, hyena_in, filters, attn_in, out_weight, attn_weight):
    hyena = hyena_in.transpose(1, 0, 2)
    attn = attn_in.transpose(1, 0, 2)
    _, rows, width = attn.shape
    taps = filters.shape[0]
    piece = out_weight.shape[1]
    n_ctx = lax.axis_size("ctx")
    slots = window // rows
    n_x = slots // 2
    n_y = n_ctx // (2 * slots)
    columns = piece * n_ctx
    dest_w = columns // n_tp
    heads = width // HEAD_DIM
    n_w = 2 + 2 * n_x + 2 * n_y
    dma = pltpu.SemaphoreType.DMA
    result = jax.ShapeDtypeStruct((rows, dest_w), BF16)
    return pl.pallas_call(
        functools.partial(kernel, window),
        out_shape=(result, result),
        in_specs=[pl.BlockSpec(memory_space=pltpu.VMEM)] * 5,
        out_specs=(pl.BlockSpec(memory_space=pltpu.VMEM),) * 2,
        scratch_shapes=[
            pltpu.VMEM((2, slots, rows, width), BF16),
            pltpu.VMEM((2, columns, width), BF16),
            pltpu.VMEM((2, n_tp, rows, dest_w), BF16),
            pltpu.VMEM((2, n_tp, rows, dest_w), BF16),
            pltpu.VMEM((2, n_tp, rows, dest_w), BF16),
            pltpu.VMEM((2, taps, width), BF16),
            pltpu.VMEM((taps + rows, width), F32),
            pltpu.VMEM((8, taps + rows, 128), F32),
            pltpu.VMEM((rows, width), BF16),
            pltpu.VMEM((rows, (slots + 1) * rows), F32),
            dma((heads, slots)),
            dma((heads, 2 * n_x)),
            dma((n_w,)),
            dma((n_w,)),
            dma((2, 2, n_tp, GROUPS)),
            dma((2, 2, n_tp, GROUPS)),
            dma((2,)),
            dma((2,)),
        ],
        compiler_params=pltpu.CompilerParams(
            collective_id=0, has_side_effects=True, vmem_limit_bytes=60 * 2**20
        ),
    )(hyena, filters, attn, out_weight.T, attn_weight.T)


def build(mesh, window):
    in_specs = (
        P("ctx", None, "tp"),
        P(None, "tp"),
        P("ctx", None, "tp"),
        P("tp", "ctx"),
        P("tp", "ctx"),
    )
    return jax.shard_map(
        functools.partial(per_device, window, mesh.shape["tp"]),
        mesh=mesh,
        in_specs=in_specs,
        out_specs=(P("ctx", "tp"), P("ctx", "tp")),
        check_vma=False,
    )


def solution(mesh):
    return build(mesh, WINDOW)
```

```python
import functools
import math

import jax
import jax.numpy as jnp
from jax import lax
from jax.experimental import pallas as pl
from jax.experimental.pallas import tpu as pltpu
from jax.sharding import PartitionSpec as P

HEAD_DIM = 128
WINDOW = 2048
GROUPS = 2
F32 = jnp.float32
BF16 = jnp.bfloat16


def kernel(
    window,
    hyena,
    filters,
    attn,
    w_hyena,
    w_attn,
    out_h,
    out_a,
    kv,
    wg,
    part,
    from_left,
    from_right,
    rim,
    padded,
    shifted,
    act,
    scores,
    kv_recv,
    kv_send,
    w_recv,
    w_send,
    rs_recv,
    rs_send,
    rim_recv,
    rim_send,
):
    _, rows, width = attn.shape
    heads = width // HEAD_DIM
    taps = filters.shape[0]
    n_ctx = lax.axis_size("ctx")
    n_tp = lax.axis_size("tp")
    slots = window // rows
    n_x = slots // 2
    n_y = n_ctx // (2 * slots)
    piece = w_hyena.shape[0]
    pair = 2 * piece
    row_w = slots * piece
    dest_w = out_h.shape[1]
    half = rows // GROUPS

    me = lax.axis_index("ctx")
    t = lax.axis_index("tp")
    row = me // slots
    i = me % slots
    y = row // 2
    zh = row % 2
    x = i // 2
    k = i % 2
    n_rows = n_ctx // slots

    def at(y_, zh_, x_, k_):
        return ((y_ * 2 + zh_) * n_x + x_) * 2 + k_

    partner = at(y, zh, x, 1 - k)
    flip = at(y, 1 - zh, x, k)
    row_next = lax.rem(row + 1, n_rows) * slots + i
    row_prev = lax.rem(row + n_rows - 1, n_rows) * slots + i
    after = lax.rem(me + 1, n_ctx)
    before = lax.rem(me + n_ctx - 1, n_ctx)
    x_peer = [at(y, zh, lax.rem(x + d, n_x), k) for d in range(1, n_x)]
    y_peer = [at(lax.rem(y + d, n_y), zh, x, k) for d in range(1, n_y)]

    barrier = pltpu.get_barrier_semaphore()
    peers = [partner, flip, row_next, row_prev, after, before] + x_peer + y_peer
    for peer in peers:
        pl.semaphore_signal(barrier, inc=1, device_id={"ctx": peer})

    @pl.when(t > 0)
    def _():
        pl.semaphore_signal(barrier, inc=1, device_id={"tp": t - 1})

    @pl.when(t < n_tp - 1)
    def _():
        pl.semaphore_signal(barrier, inc=1, device_id={"tp": t + 1})

    beside = (t > 0).astype(jnp.int32) + (t < n_tp - 1).astype(jnp.int32)
    pl.semaphore_wait(barrier, len(peers) + beside)

    def remote(src, dst, send, recv, peer, axis="ctx"):
        return pltpu.make_async_remote_copy(
            src_ref=src, dst_ref=dst, send_sem=send, recv_sem=recv, device_id={axis: peer}
        )

    def lanes(h):
        return pl.ds(pl.multiple_of(h * HEAD_DIM, HEAD_DIM), HEAD_DIM)

    def own_kv(h):
        return attn.at[pl.ds(1, 2), :, lanes(h)]

    def slot_kv(j, h):
        return kv.at[:, j, :, lanes(h)]

    def kv_copy(src, h, j, n, peer):
        return remote(src, slot_kv(j, h), kv_send.at[h, n], kv_recv.at[h, j], peer)

    def flip_kv(h):
        return kv_copy(own_kv(h), h, i, 0, row_next)

    def along(h, d, src):
        return kv_copy(src, h, i, d, x_peer[d - 1])

    def to_partner(h, src):
        return kv_copy(src, h, i, n_x, partner)

    def came(d):
        return lax.rem(x + d, n_x) * 2 + k

    def forward(h, d):
        j = came(d)
        return kv_copy(slot_kv(j, h), h, j, n_x + d, partner)

    def start_own(h):
        for d in range(1, n_x):

            @pl.when(x + d < n_x)
            def _():
                along(h, d, own_kv(h)).start()

        @pl.when(k == 0)
        def _():
            to_partner(h, own_kv(h)).start()

    def arrived(h, j):
        pltpu.make_async_copy(slot_kv(j, h), slot_kv(j, h), kv_recv.at[h, j]).wait()

    def spread(h):
        arrived(h, i)
        for d in range(1, n_x):

            @pl.when(x + d >= n_x)
            def _():
                along(h, d, slot_kv(i, h)).start()

        @pl.when(k == 1)
        def _():
            to_partner(h, slot_kv(i, h)).start()

    def pass_on(h):
        for d in range(1, n_x):
            arrived(h, came(d))
            forward(h, d).start()

    def rest(h):
        for d in range(n_x):
            arrived(h, lax.rem(x + d, n_x) * 2 + 1 - k)

    def w_rows(first, count):
        return pl.ds(pl.multiple_of(first * piece, piece), count * piece)

    def w_block(layer, first, count):
        return wg.at[layer, w_rows(first, count)]

    def w_copy(block, n, peer):
        return remote(block, block, w_send.at[n], w_recv.at[n], peer)

    def w_swap(src):
        return remote(src, w_block(1 - k, me, 1), w_send.at[0], w_recv.at[0], partner)

    def w_landed(block, n):
        pltpu.make_async_copy(block, block, w_recv.at[n]).wait()

    chip = me - k
    chip_flip = flip - k

    def w_own(ref):
        return pltpu.make_async_copy(ref, w_block(k, me, 1), w_recv.at[1])

    def w_flip():
        return w_copy(w_block(k, chip, 2), 2, flip)

    def w_along(d, other):
        return w_copy(
            w_block(k, chip_flip if other else chip, 2), 2 + d + (n_x - 1) * other, x_peer[d - 1]
        )

    base_y = 2 + 2 * n_x - 1

    def w_up(d):
        return w_copy(w_block(k, y * 2 * slots, 2 * slots), base_y + d, y_peer[d - 1])

    base_p = base_y + n_y

    def w_hand(d):
        y_ = lax.rem(y + d, n_y)
        block = w_block(k, y_ * 2 * slots, 2 * slots)
        return w_copy(block, base_p + d, partner)

    flip_kv(0).start()
    rim_rows = pl.ds(rows - taps, taps)
    for n in range(2):
        remote(hyena.at[2 * n, rim_rows], rim.at[n], rim_send.at[n], rim_recv.at[n], after).start()

    @pl.when(k == 0)
    def _():
        w_swap(w_attn).start()
        w_own(w_hyena).start()

    @pl.when(k == 1)
    def _():
        w_swap(w_hyena).start()
        w_own(w_attn).start()

    start_own(0)
    w_landed(w_block(k, me, 1), 1)
    w_landed(w_block(k, partner, 1), 0)
    w_flip().start()
    for d in range(1, n_x):
        w_along(d, 0).start()

    @pl.loop(1, heads)
    def _(h):
        flip_kv(h).start()
        start_own(h)

    own = (hyena[0].astype(F32) * hyena[2].astype(F32)).astype(BF16).astype(F32)
    padded[pl.ds(taps, rows), :] = own
    for n in range(2):
        pltpu.make_async_copy(rim.at[n], rim.at[n], rim_recv.at[n]).wait()
    rim_product = (rim[0].astype(F32) * rim[1].astype(F32)).astype(BF16).astype(F32)
    padded[pl.ds(0, taps), :] = jnp.where(me > 0, rim_product, 0.0)

    total_rows = taps + rows

    @pl.loop(0, width // 128)
    def _(tile):
        cols = pl.ds(pl.multiple_of(tile * 128, 128), 128)
        for s in range(8):
            shifted[s, pl.ds(8, total_rows - 8), :] = padded[pl.ds(8 - s, total_rows - 8), cols]

        chunk = min(rows, 128)

        @pl.loop(0, rows // chunk)
        def _(part_row):
            first = part_row * chunk

            def eight(a, acc):
                coef = filters[pl.ds(pl.multiple_of(a * 8, 8), 8), cols]
                start = pl.multiple_of(taps + first - a * 8, 8)
                for s in range(8):
                    acc = acc + coef[s : s + 1, :] * shifted[s, pl.ds(start, chunk), :]
                return acc

            acc = lax.fori_loop(0, taps // 8, eight, jnp.zeros((chunk, 128), F32))
            at_rows = pl.ds(pl.multiple_of(first, chunk), chunk)
            act[at_rows, cols] = (hyena[1, at_rows, cols].astype(F32) * acc).astype(BF16)

    w_landed(w_block(k, chip_flip, 2), 2)
    for d in range(1, n_x):
        w_along(d, 1).start()
    spread(0)
    for d in range(1, n_x):
        x_ = lax.rem(x + n_x - d, n_x)
        w_landed(w_block(k, at(y, zh, x_, 0), 2), 2 + d)
    for d in range(1, n_x):
        x_ = lax.rem(x + n_x - d, n_x)
        w_landed(w_block(k, at(y, 1 - zh, x_, 0), 2), 2 + d + n_x - 1)
    for d in range(1, n_y):
        w_up(d).start()
    w_hand(0).start()
    pass_on(0)

    @pl.loop(1, heads)
    def _(h):
        spread(h)
        pass_on(h)

    for d in range(1, n_y):
        y_ = lax.rem(y + n_y - d, n_y)
        w_landed(w_block(k, y_ * 2 * slots, 2 * slots), base_y + d)
        w_hand(n_y - d).start()
    for d in range(n_y):
        y_ = lax.rem(y + d, n_y)
        w_landed(w_block(1 - k, y_ * 2 * slots, 2 * slots), base_p + d)

    def project(layer):
        @pl.loop(0, n_tp)
        def _(d):
            weight = wg[layer, pl.ds(pl.multiple_of(d * dest_w, dest_w), dest_w), :]
            part[layer, d] = lax.dot_general(
                act[...], weight, (((1,), (1,)), ((), ())), preferred_element_type=F32
            ).astype(BF16)

    def rs_copy(layer, way, d, g):
        piece_of = (d, pl.ds(pl.multiple_of(g * half, half), half))
        buffer = (from_left, from_right)[way]
        return remote(
            part.at[(layer,) + piece_of],
            buffer.at[(layer,) + piece_of],
            rs_send.at[layer, way, d, g],
            rs_recv.at[layer, way, d, g],
            (t + 1, t - 1)[way],
            "tp",
        )

    def rs_add(layer, way, d, g):
        piece_of = (layer, d, pl.ds(pl.multiple_of(g * half, half), half))
        buffer = (from_left, from_right)[way]
        landed = buffer.at[piece_of]
        pltpu.make_async_copy(landed, landed, rs_recv.at[layer, way, d, g]).wait()
        part[piece_of] = (part[piece_of].astype(F32) + buffer[piece_of].astype(F32)).astype(BF16)

    def rs_way(layer, way, tick):
        hops = (t, n_tp - 1 - t)[way]
        step = tick - hops
        count = (n_tp - 1 - hops) * GROUPS
        m = step // GROUPS
        d = (n_tp - 1 - m, m)[way]
        g = step % GROUPS
        live = (step >= 0) & (step < count)

        @pl.when(live & (hops > 0))
        def _():
            rs_add(layer, way, d, g)

        @pl.when(live)
        def _():
            rs_copy(layer, way, d, g).start()

    def rs_step(layer, tick):
        rs_way(layer, 0, tick)
        rs_way(layer, 1, tick)

    rs_steps = (n_tp - 1) * GROUPS

    def finish(layer, out):
        total = part[layer, t].astype(F32)
        for way in range(2):

            @pl.when((t > 0) if way == 0 else (t < n_tp - 1))
            def _():
                for g in range(GROUPS):
                    buffer = (from_left, from_right)[way]
                    landed = buffer.at[layer, t, pl.ds(g * half, half)]
                    pltpu.make_async_copy(landed, landed, rs_recv.at[layer, way, t, g]).wait()

        left = jnp.where(t > 0, from_left[layer, t].astype(F32), 0.0)
        right = jnp.where(t < n_tp - 1, from_right[layer, t].astype(F32), 0.0)
        out[...] = (total + left + right).astype(BF16)

    project(0)

    scale = 1.0 / math.sqrt(HEAD_DIM)
    gap = lax.broadcasted_iota(jnp.int32, (rows, rows), 1) - lax.broadcasted_iota(
        jnp.int32, (rows, rows), 0
    )

    def attend(h):
        queries = attn[0, :, lanes(h)]

        def block_scores(keys):
            return (
                lax.dot_general(
                    queries, keys, (((1,), (1,)), ((), ())), preferred_element_type=F32
                )
                * scale
            )

        def fold(op, block):
            kept = block[:, :128]
            for n in range(1, rows // 128):
                kept = op(kept, block[:, n * 128 : (n + 1) * 128])
            return kept

        own = jnp.where(gap <= 0, block_scores(attn[1, :, lanes(h)]), -jnp.inf)
        scores[:, slots * rows :] = own
        top = fold(jnp.maximum, own)
        for j in range(slots):
            least = jnp.where(i == j, 0, -rows)
            least = jnp.where((row == 0) & (i <= j), rows, least)
            block = jnp.where(gap > least, block_scores(kv[0, j, :, lanes(h)]), -jnp.inf)
            scores[:, j * rows : (j + 1) * rows] = block
            top = jnp.maximum(top, fold(jnp.maximum, block))
        top = jnp.max(top, axis=1, keepdims=True)
        total = jnp.zeros((rows, 128), F32)
        result = jnp.zeros((rows, HEAD_DIM), F32)
        for j in range(slots + 1):
            weights = jnp.exp(scores[:, j * rows : (j + 1) * rows] - top)
            total = total + fold(jnp.add, weights)
            values = attn[2, :, lanes(h)] if j == slots else kv[1, j, :, lanes(h)]
            result = result + jnp.dot(weights.astype(BF16), values, preferred_element_type=F32)
        total = jnp.sum(total, axis=1, keepdims=True)
        act[:, lanes(h)] = (result / total).astype(BF16)

    per_head = -(-rs_steps // heads)

    @pl.loop(0, heads)
    def _(h):
        rest(h)
        attend(h)

        @pl.loop(h * per_head, jnp.minimum((h + 1) * per_head, rs_steps))
        def _(step):
            rs_step(0, step)

    project(1)

    @pl.loop(0, rs_steps)
    def _(step):
        rs_step(1, step)

    finish(0, out_h)
    finish(1, out_a)

    for n in range(2):
        remote(hyena.at[2 * n, rim_rows], rim.at[n], rim_send.at[n], rim_recv.at[n], after).wait_send()
    w_swap(w_attn).wait_send()
    w_flip().wait_send()
    for d in range(1, n_x):
        w_along(d, 0).wait_send()
        w_along(d, 1).wait_send()
    for d in range(1, n_y):
        w_up(d).wait_send()
    for d in range(n_y):
        w_hand(d).wait_send()

    @pl.loop(0, heads)
    def _(h):
        flip_kv(h).wait_send()
        for d in range(1, n_x):
            along(h, d, own_kv(h)).wait_send()
            forward(h, d).wait_send()
        to_partner(h, own_kv(h)).wait_send()

    @pl.loop(0, rs_steps)
    def _(step):
        m = step // GROUPS
        g = step % GROUPS
        for layer in range(2):

            @pl.when(t < n_tp - 1 - m)
            def _():
                rs_copy(layer, 0, n_tp - 1 - m, g).wait_send()

            @pl.when(t > m)
            def _():
                rs_copy(layer, 1, m, g).wait_send()


def per_device(window, n_tp, hyena_in, filters, attn_in, out_weight, attn_weight):
    hyena = hyena_in.transpose(1, 0, 2)
    attn = attn_in.transpose(1, 0, 2)
    _, rows, width = attn.shape
    taps = filters.shape[0]
    piece = out_weight.shape[1]
    n_ctx = lax.axis_size("ctx")
    slots = window // rows
    n_x = slots // 2
    n_y = n_ctx // (2 * slots)
    columns = piece * n_ctx
    dest_w = columns // n_tp
    heads = width // HEAD_DIM
    n_w = 2 + 2 * n_x + 2 * n_y
    dma = pltpu.SemaphoreType.DMA
    result = jax.ShapeDtypeStruct((rows, dest_w), BF16)
    return pl.pallas_call(
        functools.partial(kernel, window),
        out_shape=(result, result),
        in_specs=[pl.BlockSpec(memory_space=pltpu.VMEM)] * 5,
        out_specs=(pl.BlockSpec(memory_space=pltpu.VMEM),) * 2,
        scratch_shapes=[
            pltpu.VMEM((2, slots, rows, width), BF16),
            pltpu.VMEM((2, columns, width), BF16),
            pltpu.VMEM((2, n_tp, rows, dest_w), BF16),
            pltpu.VMEM((2, n_tp, rows, dest_w), BF16),
            pltpu.VMEM((2, n_tp, rows, dest_w), BF16),
            pltpu.VMEM((2, taps, width), BF16),
            pltpu.VMEM((taps + rows, width), F32),
            pltpu.VMEM((8, taps + rows, 128), F32),
            pltpu.VMEM((rows, width), BF16),
            pltpu.VMEM((rows, (slots + 1) * rows), F32),
            dma((heads, slots)),
            dma((heads, 2 * n_x)),
            dma((n_w,)),
            dma((n_w,)),
            dma((2, 2, n_tp, GROUPS)),
            dma((2, 2, n_tp, GROUPS)),
            dma((2,)),
            dma((2,)),
        ],
        compiler_params=pltpu.CompilerParams(
            collective_id=0, has_side_effects=True, vmem_limit_bytes=60 * 2**20
        ),
    )(hyena, filters, attn, out_weight.T, attn_weight.T)


def build(mesh, window):
    in_specs = (
        P("ctx", None, "tp"),
        P(None, "tp"),
        P("ctx", None, "tp"),
        P("tp", "ctx"),
        P("tp", "ctx"),
    )
    return jax.shard_map(
        functools.partial(per_device, window, mesh.shape["tp"]),
        mesh=mesh,
        in_specs=in_specs,
        out_specs=(P("ctx", "tp"), P("ctx", "tp")),
        check_vma=False,
    )


def solution(mesh):
    return build(mesh, WINDOW)
```

```python
import functools
import math

import jax
import jax.numpy as jnp
from jax import lax
from jax.experimental import pallas as pl
from jax.experimental.pallas import tpu as pltpu
from jax.sharding import PartitionSpec as P

HEAD_DIM = 128
WINDOW = 2048
GROUPS = 2
F32 = jnp.float32
BF16 = jnp.bfloat16


def kernel(
    window,
    hyena,
    filters,
    attn,
    w_hyena,
    w_attn,
    out_h,
    out_a,
    kv,
    wg,
    w_far,
    w_share,
    wa,
    gathered,
    part,
    from_left,
    from_right,
    rim_out,
    rim,
    padded,
    shifted,
    act,
    scores,
    kv_recv,
    kv_send,
    w_recv,
    w_send,
    rs_recv,
    rs_send,
    rim_recv,
    rim_send,
    wa_recv,
    wa_send,
    ag_recv,
    ag_send,
):
    _, rows, width = attn.shape
    heads = width // HEAD_DIM
    taps = filters.shape[0]
    n_ctx = lax.axis_size("ctx")
    n_tp = lax.axis_size("tp")
    slots = window // rows
    n_x = slots // 2
    n_y = n_ctx // (2 * slots)
    piece = w_hyena.shape[0]
    pair = 2 * piece
    row_w = slots * piece
    dest_w = out_h.shape[1]
    half = rows // GROUPS

    me = lax.axis_index("ctx")
    t = lax.axis_index("tp")
    row = me // slots
    i = me % slots
    y = row // 2
    zh = row % 2
    x = i // 2
    k = i % 2
    n_rows = n_ctx // slots

    def at(y_, zh_, x_, k_):
        return ((y_ * 2 + zh_) * n_x + x_) * 2 + k_

    partner = at(y, zh, x, 1 - k)
    flip = at(y, 1 - zh, x, k)
    row_next = lax.rem(row + 1, n_rows) * slots + i
    row_prev = lax.rem(row + n_rows - 1, n_rows) * slots + i
    after = lax.rem(me + 1, n_ctx)
    before = lax.rem(me + n_ctx - 1, n_ctx)
    x_peer = [at(y, zh, lax.rem(x + d, n_x), k) for d in range(1, n_x)]
    y_peer = [at(lax.rem(y + d, n_y), zh, x, k) for d in range(1, n_y)]

    barrier = pltpu.get_barrier_semaphore()
    peers = [partner, flip, row_next, row_prev, after, before] + x_peer + y_peer
    for peer in peers:
        pl.semaphore_signal(barrier, inc=1, device_id={"ctx": peer})

    @pl.when(t > 0)
    def _():
        pl.semaphore_signal(barrier, inc=1, device_id={"tp": t - 1})

    @pl.when(t < n_tp - 1)
    def _():
        pl.semaphore_signal(barrier, inc=1, device_id={"tp": t + 1})

    beside = (t > 0).astype(jnp.int32) + (t < n_tp - 1).astype(jnp.int32)

    holder = t % 2 == zh

    @pl.when(holder)
    def _():
        for s in range(n_tp):

            @pl.when(s != t)
            def _():
                pl.semaphore_signal(barrier, inc=1, device_id={"tp": s})

    collectors = n_tp // 2 - holder.astype(jnp.int32)
    pl.semaphore_wait(barrier, len(peers) + beside + collectors)

    def remote(src, dst, send, recv, peer, axis="ctx"):
        return pltpu.make_async_remote_copy(
            src_ref=src, dst_ref=dst, send_sem=send, recv_sem=recv, device_id={axis: peer}
        )

    def lanes(h):
        return pl.ds(pl.multiple_of(h * HEAD_DIM, HEAD_DIM), HEAD_DIM)

    def own_kv(h):
        return attn.at[pl.ds(1, 2), :, lanes(h)]

    def slot_kv(j, h):
        return kv.at[:, j, :, lanes(h)]

    def kv_copy(src, h, j, n, peer):
        return remote(src, slot_kv(j, h), kv_send.at[h, n], kv_recv.at[h, j], peer)

    def flip_kv(h):
        return kv_copy(own_kv(h), h, i, 0, row_next)

    def along(h, d, src):
        return kv_copy(src, h, i, d, x_peer[d - 1])

    def to_partner(h, src):
        return kv_copy(src, h, i, n_x, partner)

    def came(d):
        return lax.rem(x + d, n_x) * 2 + k

    def forward(h, d):
        j = came(d)
        return kv_copy(slot_kv(j, h), h, j, n_x + d, partner)

    def start_own(h):
        for d in range(1, n_x):

            @pl.when(x + d < n_x)
            def _():
                along(h, d, own_kv(h)).start()

        @pl.when(k == 0)
        def _():
            to_partner(h, own_kv(h)).start()

    def arrived(h, j):
        pltpu.make_async_copy(slot_kv(j, h), slot_kv(j, h), kv_recv.at[h, j]).wait()

    def spread(h):
        arrived(h, i)
        for d in range(1, n_x):

            @pl.when(x + d >= n_x)
            def _():
                along(h, d, slot_kv(i, h)).start()

        @pl.when(k == 1)
        def _():
            to_partner(h, slot_kv(i, h)).start()

    def pass_on(h):
        for d in range(1, n_x):
            arrived(h, came(d))
            forward(h, d).start()

    def rest(h):
        for d in range(n_x):
            arrived(h, lax.rem(x + d, n_x) * 2 + 1 - k)

    side_w = width // 2

    def side(k_):
        return pl.ds(pl.multiple_of(k_ * side_w, side_w), side_w)

    def w_rows(first, count):
        return pl.ds(pl.multiple_of(first * piece, piece), count * piece)

    def w_block(k_, first, count):
        return wg.at[w_rows(first, count), side(k_)]

    def w_copy(block, n, peer):
        return remote(block, block, w_send.at[n], w_recv.at[n], peer)

    def w_swap(src, owner, n):
        return remote(
            src.at[:, side(1 - k)], w_block(1 - k, owner, 1), w_send.at[n], w_recv.at[n], partner
        )

    def w_keep(src, owner, n):
        return pltpu.make_async_copy(src.at[:, side(k)], w_block(k, owner, 1), w_recv.at[n])

    def w_landed(block, n):
        pltpu.make_async_copy(block, block, w_recv.at[n]).wait()

    chip = me - k
    chip_flip = flip - k

    last = 2 + 2 * n_x + 2 * n_y

    def w_flip():
        return remote(w_hyena, w_far, w_send.at[2], w_recv.at[2], flip)

    def w_along(d, other):
        return w_copy(
            w_block(k, chip_flip if other else chip, 2), 2 + d + (n_x - 1) * other, x_peer[d - 1]
        )

    base_y = 2 + 2 * n_x - 1

    def w_up(d):
        return w_copy(w_block(k, y * 2 * slots, 2 * slots), base_y + d, y_peer[d - 1])

    base_p = base_y + n_y

    def w_hand(d):
        y_ = lax.rem(y + d, n_y)
        block = w_block(k, y_ * 2 * slots, 2 * slots)
        return w_copy(block, base_p + d, partner)

    share = piece // n_y

    def wa_part(j, y_):
        return pl.ds(pl.multiple_of(j * piece + y_ * share, share), share)

    def wa_block(j):
        return wa.at[:, w_rows(j, 1)]

    def wa_scatter(d):
        y_ = lax.rem(y + d, n_y)
        src = w_attn.at[pl.ds(pl.multiple_of(y_ * share, share), share)]
        return remote(src, w_share.at[y], wa_send.at[d], wa_recv.at[y], y_peer[d - 1])

    def wa_keep():
        src = w_attn.at[pl.ds(pl.multiple_of(y * share, share), share)]
        return pltpu.make_async_copy(src, w_share.at[y], wa_recv.at[y])

    def wa_line(y_):
        return remote(
            w_share.at[y_],
            wa.at[t, wa_part(i, y)],
            wa_send.at[n_y + y_],
            wa_recv.at[n_y + t],
            2 * y_ + zh,
            "tp",
        )

    def wa_own(y_):
        return pltpu.make_async_copy(
            w_share.at[y_], wa.at[t, wa_part(i, y)], wa_recv.at[n_y + t]
        )

    def wa_flip():
        block = wa.at[:, wa_part(i, y)]
        return remote(block, block, wa_send.at[2 * n_y], wa_recv.at[n_y + n_tp], flip)

    def wa_up(d):
        block = wa.at[:, wa_part(i, y)]
        return remote(
            block, block, wa_send.at[2 * n_y + d], wa_recv.at[n_y + n_tp + d], y_peer[d - 1]
        )

    def wa_along(d):
        block = wa_block(i)
        return remote(
            block, block, wa_send.at[3 * n_y + d], wa_recv.at[2 * n_y + n_tp + d], x_peer[d - 1]
        )

    def wa_hand(d):
        block = wa_block(lax.rem(x + d, n_x) * 2 + k)
        n = n_x + d
        return remote(
            block, block, wa_send.at[3 * n_y + n], wa_recv.at[2 * n_y + n_tp + n], partner
        )

    def wa_landed(block, n):
        pltpu.make_async_copy(block, block, wa_recv.at[n]).wait()

    def wa_send_lines():
        for y_ in range(n_y):
            wa_landed(w_share.at[y_], y_)
        for y_ in range(n_y):

            @pl.when(2 * y_ + zh != t)
            def _():
                wa_line(y_).start()

            @pl.when(2 * y_ + zh == t)
            def _():
                wa_own(y_).start()

    def wa_collect():
        @pl.when(holder)
        def _():
            for s in range(n_tp):
                wa_landed(wa.at[s, wa_part(i, y)], n_y + s)
            wa_flip().start()
            for d in range(1, n_y):
                wa_up(d).start()

    def wa_spread():
        @pl.when(jnp.logical_not(holder))
        def _():
            wa_landed(wa.at[:, wa_part(i, y)], n_y + n_tp)
            for d in range(1, n_y):
                wa_up(d).start()

    def wa_rows_done():
        for d in range(1, n_y):
            wa_landed(wa.at[:, wa_part(i, lax.rem(y + n_y - d, n_y))], n_y + n_tp + d)
        for d in range(1, n_x):
            wa_along(d).start()
        wa_hand(0).start()

    def wa_hand_on():
        for d in range(1, n_x):
            j = lax.rem(x + n_x - d, n_x) * 2 + k
            wa_landed(wa_block(j), 2 * n_y + n_tp + d)
            wa_hand(n_x - d).start()

    def wa_done():
        for d in range(n_x):
            j = lax.rem(x + d, n_x) * 2 + 1 - k
            wa_landed(wa_block(j), 2 * n_y + n_tp + n_x + d)

    product = (hyena[0].astype(F32) * hyena[2].astype(F32)).astype(BF16)
    rim_out[...] = product[rows - taps :]

    def rim_copy():
        return remote(rim_out, rim, rim_send, rim_recv, after)

    w_flip().start()
    rim_copy().start()
    w_swap(w_hyena, me, 0).start()
    w_keep(w_hyena, me, 1).start()

    for d in range(1, n_y):
        wa_scatter(d).start()
    wa_keep().start()

    @pl.loop(0, heads)
    def _(h):
        flip_kv(h).start()
        start_own(h)

    w_landed(w_block(k, me, 1), 1)
    w_landed(w_block(k, partner, 1), 0)
    for d in range(1, n_x):
        w_along(d, 0).start()

    padded[pl.ds(taps, rows), :] = product.astype(F32)
    chunk = rows // 2

    def convolve(first):
        low = max(first - 8 * (taps // 8 - 1) + taps, 8)
        count = first + taps + chunk - low

        @pl.loop(0, width // 128)
        def _(tile):
            cols = pl.ds(pl.multiple_of(tile * 128, 128), 128)
            for s in range(8):
                shifted[s, pl.ds(low, count), :] = padded[pl.ds(low - s, count), cols]

            def eight(a, acc):
                coef = filters[pl.ds(pl.multiple_of(a * 8, 8), 8), cols]
                start = pl.multiple_of(taps + first - a * 8, 8)
                for s in range(8):
                    acc = acc + coef[s : s + 1, :] * shifted[s, pl.ds(start, chunk), :]
                return acc

            acc = lax.fori_loop(0, taps // 8, eight, jnp.zeros((chunk, 128), F32))
            gate = hyena[1, pl.ds(first, chunk), cols].astype(F32)
            act[pl.ds(first, chunk), cols] = (gate * acc).astype(BF16)

    if chunk >= taps:
        convolve(chunk)
    wa_send_lines()
    w_landed(w_far, 2)
    w_swap(w_far, flip, last).start()
    w_keep(w_far, flip, last + 1).start()
    w_landed(w_block(k, flip, 1), last + 1)
    w_landed(w_block(k, at(y, 1 - zh, x, 1 - k), 1), last)
    for d in range(1, n_x):
        w_along(d, 1).start()
    for d in range(1, n_x):
        x_ = lax.rem(x + n_x - d, n_x)
        w_landed(w_block(k, at(y, zh, x_, 0), 2), 2 + d)
    for d in range(1, n_x):
        x_ = lax.rem(x + n_x - d, n_x)
        w_landed(w_block(k, at(y, 1 - zh, x_, 0), 2), 2 + d + n_x - 1)
    for d in range(1, n_y):
        w_up(d).start()
    w_hand(0).start()
    spread(0)

    @pl.loop(0, heads // 2)
    def _(h):
        spread(h + 1)
        pass_on(h)

    for d in range(1, n_y):
        y_ = lax.rem(y + n_y - d, n_y)
        w_landed(w_block(k, y_ * 2 * slots, 2 * slots), base_y + d)
        w_hand(n_y - d).start()

    wa_collect()

    @pl.loop(heads // 2, heads)
    def _(h):
        @pl.when(h < heads - 1)
        def _():
            spread(h + 1)

        pass_on(h)

    pltpu.make_async_copy(rim, rim, rim_recv).wait()
    padded[pl.ds(0, taps), :] = jnp.where(me > 0, rim[...].astype(F32), 0.0)
    convolve(0)
    if chunk < taps:
        convolve(chunk)

    for d in range(n_y):
        y_ = lax.rem(y + d, n_y)
        w_landed(w_block(1 - k, y_ * 2 * slots, 2 * slots), base_p + d)

    @pl.loop(0, n_tp)
    def _(d):
        weight = wg[pl.ds(pl.multiple_of(d * dest_w, dest_w), dest_w), :]
        part[d] = lax.dot_general(
            act[...], weight, (((1,), (1,)), ((), ())), preferred_element_type=F32
        ).astype(BF16)

    wa_spread()

    def rs_copy(way, d, g):
        piece_of = (d, pl.ds(pl.multiple_of(g * half, half), half))
        buffer = (from_left, from_right)[way]
        return remote(
            part.at[piece_of],
            buffer.at[piece_of],
            rs_send.at[way, d, g],
            rs_recv.at[way, d, g],
            (t + 1, t - 1)[way],
            "tp",
        )

    def rs_add(way, d, g):
        piece_of = (d, pl.ds(pl.multiple_of(g * half, half), half))
        buffer = (from_left, from_right)[way]
        landed = buffer.at[piece_of]
        pltpu.make_async_copy(landed, landed, rs_recv.at[way, d, g]).wait()
        part[piece_of] = (part[piece_of].astype(F32) + buffer[piece_of].astype(F32)).astype(BF16)

    def rs_way(way, tick):
        hops = (t, n_tp - 1 - t)[way]
        step = tick - hops
        count = (n_tp - 1 - hops) * GROUPS
        m = step // GROUPS
        d = (n_tp - 1 - m, m)[way]
        g = step % GROUPS
        live = (step >= 0) & (step < count)

        @pl.when(live & (hops > 0))
        def _():
            rs_add(way, d, g)

        @pl.when(live)
        def _():
            rs_copy(way, d, g).start()

    def rs_step(tick):
        rs_way(0, tick)
        rs_way(1, tick)

    rs_steps = (n_tp - 1) * GROUPS

    def finish(out):
        total = part[t].astype(F32)
        for way in range(2):

            @pl.when((t > 0) if way == 0 else (t < n_tp - 1))
            def _():
                for g in range(GROUPS):
                    buffer = (from_left, from_right)[way]
                    landed = buffer.at[t, pl.ds(g * half, half)]
                    pltpu.make_async_copy(landed, landed, rs_recv.at[way, t, g]).wait()

        left = jnp.where(t > 0, from_left[t].astype(F32), 0.0)
        right = jnp.where(t < n_tp - 1, from_right[t].astype(F32), 0.0)
        out[...] = (total + left + right).astype(BF16)

    scale = 1.0 / math.sqrt(HEAD_DIM)
    gap = lax.broadcasted_iota(jnp.int32, (rows, rows), 1) - lax.broadcasted_iota(
        jnp.int32, (rows, rows), 0
    )

    def attend(h):
        queries = attn[0, :, lanes(h)]

        def block_scores(keys):
            return (
                lax.dot_general(
                    queries, keys, (((1,), (1,)), ((), ())), preferred_element_type=F32
                )
                * scale
            )

        def fold(op, block):
            kept = block[:, :128]
            for n in range(1, rows // 128):
                kept = op(kept, block[:, n * 128 : (n + 1) * 128])
            return kept

        own = jnp.where(gap <= 0, block_scores(attn[1, :, lanes(h)]), -jnp.inf)
        scores[:, slots * rows :] = own
        top = fold(jnp.maximum, own)
        for j in range(slots):
            least = jnp.where(i == j, 0, -rows)
            least = jnp.where((row == 0) & (i <= j), rows, least)
            block = jnp.where(gap > least, block_scores(kv[0, j, :, lanes(h)]), -jnp.inf)
            scores[:, j * rows : (j + 1) * rows] = block
            top = jnp.maximum(top, fold(jnp.maximum, block))
        top = jnp.max(top, axis=1, keepdims=True)
        total = jnp.zeros((rows, 128), F32)
        result = jnp.zeros((rows, HEAD_DIM), F32)
        for j in range(slots + 1):
            weights = jnp.exp(scores[:, j * rows : (j + 1) * rows] - top)
            total = total + fold(jnp.add, weights)
            values = attn[2, :, lanes(h)] if j == slots else kv[1, j, :, lanes(h)]
            result = result + jnp.dot(weights.astype(BF16), values, preferred_element_type=F32)
        total = jnp.sum(total, axis=1, keepdims=True)
        gathered[t, :, lanes(h)] = (result / total).astype(BF16)

    def ag_copy(h, way, s):
        block = gathered.at[s, :, lanes(h)]
        return remote(
            block, block, ag_send.at[h, way, s], ag_recv.at[h, s], (t + 1, t - 1)[way], "tp"
        )

    def ag_step(h, hops):
        for way in range(2):
            s = (t - hops, t + hops)[way]
            live = (s >= 0, s < n_tp)[way]
            more = (t < n_tp - 1, t > 0)[way]

            @pl.when(live & (hops > 0))
            def _():
                block = gathered.at[s, :, lanes(h)]
                pltpu.make_async_copy(block, block, ag_recv.at[h, s]).wait()

            @pl.when(live & more)
            def _():
                ag_copy(h, way, s).start()

    def add_source(s):
        scores[:, :dest_w] += lax.dot_general(
            gathered[s], wa[s], (((1,), (1,)), ((), ())), preferred_element_type=F32
        )

    def rs_pair(n):
        @pl.loop(2 * n, jnp.minimum(2 * n + 2, rs_steps))
        def _(tick):
            rs_step(tick)

    @pl.loop(0, heads // 2)
    def _(n):
        rest(n)
        attend(n)

        @pl.loop(0, n + 1)
        def _(hops):
            ag_step(n - hops, hops)

        rs_pair(n)

    wa_rows_done()

    @pl.loop(heads // 2, heads)
    def _(n):
        rest(n)
        attend(n)

        @pl.loop(0, n + 1)
        def _(hops):
            ag_step(n - hops, hops)

        rs_pair(n)

    wa_hand_on()
    wa_done()
    scores[:, :dest_w] = jnp.zeros((rows, dest_w), F32)
    add_source(t)

    @pl.loop(heads, heads + n_tp - 1)
    def _(n):
        @pl.loop(jnp.maximum(n - n_tp + 1, 0), heads)
        def _(h):
            ag_step(h, n - h)

        rs_pair(n)
        hops = n - heads + 1

        @pl.when(t >= hops)
        def _():
            add_source(t - hops)

        @pl.when(t + hops < n_tp)
        def _():
            add_source(t + hops)

    out_a[...] = scores[:, :dest_w].astype(BF16)
    finish(out_h)

    rim_copy().wait_send()
    w_swap(w_hyena, me, 0).wait_send()
    w_swap(w_far, flip, last).wait_send()
    w_flip().wait_send()
    for d in range(1, n_x):
        w_along(d, 0).wait_send()
        w_along(d, 1).wait_send()
    for d in range(1, n_y):
        w_up(d).wait_send()
    for d in range(n_y):
        w_hand(d).wait_send()

    @pl.loop(0, heads)
    def _(h):
        flip_kv(h).wait_send()
        for d in range(1, n_x):
            along(h, d, own_kv(h)).wait_send()
            forward(h, d).wait_send()
        to_partner(h, own_kv(h)).wait_send()

    @pl.loop(0, rs_steps)
    def _(step):
        m = step // GROUPS
        g = step % GROUPS

        @pl.when(t < n_tp - 1 - m)
        def _():
            rs_copy(0, n_tp - 1 - m, g).wait_send()

        @pl.when(t > m)
        def _():
            rs_copy(1, m, g).wait_send()

    for d in range(1, n_y):
        wa_scatter(d).wait_send()
        wa_up(d).wait_send()
    for y_ in range(n_y):

        @pl.when(2 * y_ + zh != t)
        def _():
            wa_line(y_).wait_send()

    @pl.when(holder)
    def _():
        wa_flip().wait_send()

    for d in range(1, n_x):
        wa_along(d).wait_send()
    for d in range(n_x):
        wa_hand(d).wait_send()

    @pl.loop(0, heads)
    def _(h):
        @pl.loop(0, n_tp)
        def _(s):
            @pl.when((s <= t) & (t < n_tp - 1))
            def _():
                ag_copy(h, 0, s).wait_send()

            @pl.when((s >= t) & (t > 0))
            def _():
                ag_copy(h, 1, s).wait_send()


def per_device(window, n_tp, hyena_in, filters, attn_in, out_weight, attn_weight):
    hyena = hyena_in.transpose(1, 0, 2)
    attn = attn_in.transpose(1, 0, 2)
    _, rows, width = attn.shape
    taps = filters.shape[0]
    piece = out_weight.shape[1]
    n_ctx = lax.axis_size("ctx")
    slots = window // rows
    n_x = slots // 2
    n_y = n_ctx // (2 * slots)
    columns = piece * n_ctx
    dest_w = columns // n_tp
    heads = width // HEAD_DIM
    n_w = 4 + 2 * n_x + 2 * n_y
    dma = pltpu.SemaphoreType.DMA
    result = jax.ShapeDtypeStruct((rows, dest_w), BF16)
    return pl.pallas_call(
        functools.partial(kernel, window),
        out_shape=(result, result),
        in_specs=[pl.BlockSpec(memory_space=pltpu.VMEM)] * 5,
        out_specs=(pl.BlockSpec(memory_space=pltpu.VMEM),) * 2,
        scratch_shapes=[
            pltpu.VMEM((2, slots, rows, width), BF16),
            pltpu.VMEM((columns, width), BF16),
            pltpu.VMEM((piece, width), BF16),
            pltpu.VMEM((n_y, piece // n_y, width), BF16),
            pltpu.VMEM((n_tp, dest_w, width), BF16),
            pltpu.VMEM((n_tp, rows, width), BF16),
            pltpu.VMEM((n_tp, rows, dest_w), BF16),
            pltpu.VMEM((n_tp, rows, dest_w), BF16),
            pltpu.VMEM((n_tp, rows, dest_w), BF16),
            pltpu.VMEM((taps, width), BF16),
            pltpu.VMEM((taps, width), BF16),
            pltpu.VMEM((taps + rows, width), F32),
            pltpu.VMEM((8, taps + rows, 128), F32),
            pltpu.VMEM((rows, width), BF16),
            pltpu.VMEM((rows, (slots + 1) * rows), F32),
            dma((heads, slots)),
            dma((heads, 2 * n_x)),
            dma((n_w,)),
            dma((n_w,)),
            dma((2, n_tp, GROUPS)),
            dma((2, n_tp, GROUPS)),
            dma,
            dma,
            dma((n_tp + 2 * n_y + 2 * n_x,)),
            dma((3 * n_y + 2 * n_x,)),
            dma((heads, n_tp)),
            dma((heads, 2, n_tp)),
        ],
        compiler_params=pltpu.CompilerParams(
            collective_id=0, has_side_effects=True, vmem_limit_bytes=60 * 2**20
        ),
    )(hyena, filters, attn, out_weight.T, attn_weight.T)


def build(mesh, window):
    in_specs = (
        P("ctx", None, "tp"),
        P(None, "tp"),
        P("ctx", None, "tp"),
        P("tp", "ctx"),
        P("tp", "ctx"),
    )
    return jax.shard_map(
        functools.partial(per_device, window, mesh.shape["tp"]),
        mesh=mesh,
        in_specs=in_specs,
        out_specs=(P("ctx", "tp"), P("ctx", "tp")),
        check_vma=False,
    )


def solution(mesh):
    return build(mesh, WINDOW)
```

```python
import functools
import math

import jax
import jax.numpy as jnp
from jax import lax
from jax.experimental import pallas as pl
from jax.experimental.pallas import tpu as pltpu
from jax.sharding import PartitionSpec as P

HEAD_DIM = 128
WINDOW = 2048
GROUPS = 2
F32 = jnp.float32
BF16 = jnp.bfloat16


def kernel(
    window,
    hyena,
    filters,
    attn,
    w_hyena,
    w_attn,
    out_h,
    out_a,
    kv,
    wg,
    w_far,
    w_share,
    wa,
    gathered,
    part,
    from_left,
    from_right,
    rim_out,
    rim,
    padded,
    shifted,
    act,
    scores,
    kv_recv,
    kv_send,
    w_recv,
    w_send,
    rs_recv,
    rs_send,
    rim_recv,
    rim_send,
    wa_recv,
    wa_send,
    ag_recv,
    ag_send,
):
    _, rows, width = attn.shape
    heads = width // HEAD_DIM
    taps = filters.shape[0]
    n_ctx = lax.axis_size("ctx")
    n_tp = lax.axis_size("tp")
    slots = window // rows
    n_x = slots // 2
    n_y = n_ctx // (2 * slots)
    piece = w_hyena.shape[0]
    pair = 2 * piece
    row_w = slots * piece
    dest_w = out_h.shape[1]
    half = rows // GROUPS

    me = lax.axis_index("ctx")
    t = lax.axis_index("tp")
    row = me // slots
    i = me % slots
    y = row // 2
    zh = row % 2
    x = i // 2
    k = i % 2
    n_rows = n_ctx // slots

    def at(y_, zh_, x_, k_):
        return ((y_ * 2 + zh_) * n_x + x_) * 2 + k_

    partner = at(y, zh, x, 1 - k)
    flip = at(y, 1 - zh, x, k)
    row_next = lax.rem(row + 1, n_rows) * slots + i
    row_prev = lax.rem(row + n_rows - 1, n_rows) * slots + i
    after = lax.rem(me + 1, n_ctx)
    before = lax.rem(me + n_ctx - 1, n_ctx)
    x_peer = [at(y, zh, lax.rem(x + d, n_x), k) for d in range(1, n_x)]
    y_peer = [at(lax.rem(y + d, n_y), zh, x, k) for d in range(1, n_y)]

    barrier = pltpu.get_barrier_semaphore()
    peers = [partner, flip, row_next, row_prev, after, before] + x_peer + y_peer
    for peer in peers:
        pl.semaphore_signal(barrier, inc=1, device_id={"ctx": peer})

    @pl.when(t > 0)
    def _():
        pl.semaphore_signal(barrier, inc=1, device_id={"tp": t - 1})

    @pl.when(t < n_tp - 1)
    def _():
        pl.semaphore_signal(barrier, inc=1, device_id={"tp": t + 1})

    beside = (t > 0).astype(jnp.int32) + (t < n_tp - 1).astype(jnp.int32)

    holder = t % 2 == zh

    @pl.when(holder)
    def _():
        for s in range(n_tp):

            @pl.when(s != t)
            def _():
                pl.semaphore_signal(barrier, inc=1, device_id={"tp": s})

    collectors = n_tp // 2 - holder.astype(jnp.int32)
    pl.semaphore_wait(barrier, len(peers) + beside + collectors)

    def remote(src, dst, send, recv, peer, axis="ctx"):
        return pltpu.make_async_remote_copy(
            src_ref=src, dst_ref=dst, send_sem=send, recv_sem=recv, device_id={axis: peer}
        )

    def lanes(h):
        return pl.ds(pl.multiple_of(h * HEAD_DIM, HEAD_DIM), HEAD_DIM)

    def own_kv(h):
        return attn.at[pl.ds(1, 2), :, lanes(h)]

    def slot_kv(j, h):
        return kv.at[:, j, :, lanes(h)]

    def kv_copy(src, h, j, n, peer):
        return remote(src, slot_kv(j, h), kv_send.at[h, n], kv_recv.at[h, j], peer)

    def flip_kv(h):
        return kv_copy(own_kv(h), h, i, 0, row_next)

    def along(h, d, src):
        return kv_copy(src, h, i, d, x_peer[d - 1])

    def to_partner(h, src):
        return kv_copy(src, h, i, n_x, partner)

    def came(d):
        return lax.rem(x + d, n_x) * 2 + k

    def forward(h, d):
        j = came(d)
        return kv_copy(slot_kv(j, h), h, j, n_x + d, partner)

    def start_own(h):
        for d in range(1, n_x):

            @pl.when(x + d < n_x)
            def _():
                along(h, d, own_kv(h)).start()

        @pl.when(k == 0)
        def _():
            to_partner(h, own_kv(h)).start()

    def arrived(h, j):
        pltpu.make_async_copy(slot_kv(j, h), slot_kv(j, h), kv_recv.at[h, j]).wait()

    def spread(h):
        arrived(h, i)
        for d in range(1, n_x):

            @pl.when(x + d >= n_x)
            def _():
                along(h, d, slot_kv(i, h)).start()

        @pl.when(k == 1)
        def _():
            to_partner(h, slot_kv(i, h)).start()

    def pass_on(h):
        for d in range(1, n_x):
            arrived(h, came(d))
            forward(h, d).start()

    def rest(h):
        for d in range(n_x):
            arrived(h, lax.rem(x + d, n_x) * 2 + 1 - k)

    side_w = width // 2

    def side(k_):
        return pl.ds(pl.multiple_of(k_ * side_w, side_w), side_w)

    def w_rows(first, count):
        return pl.ds(pl.multiple_of(first * piece, piece), count * piece)

    def w_block(k_, first, count):
        return wg.at[w_rows(first, count), side(k_)]

    def w_copy(block, n, peer):
        return remote(block, block, w_send.at[n], w_recv.at[n], peer)

    def w_swap(src, owner, n):
        return remote(
            src.at[:, side(1 - k)], w_block(1 - k, owner, 1), w_send.at[n], w_recv.at[n], partner
        )

    def w_keep(src, owner, n):
        return pltpu.make_async_copy(src.at[:, side(k)], w_block(k, owner, 1), w_recv.at[n])

    def w_landed(block, n):
        pltpu.make_async_copy(block, block, w_recv.at[n]).wait()

    chip = me - k
    chip_flip = flip - k

    last = 2 + 2 * n_x + 2 * n_y

    def w_flip():
        return remote(w_hyena, w_far, w_send.at[2], w_recv.at[2], flip)

    def w_along(d, other):
        return w_copy(
            w_block(k, chip_flip if other else chip, 2), 2 + d + (n_x - 1) * other, x_peer[d - 1]
        )

    base_y = 2 + 2 * n_x - 1

    def w_up(d):
        return w_copy(w_block(k, y * 2 * slots, 2 * slots), base_y + d, y_peer[d - 1])

    base_p = base_y + n_y

    def w_hand(d):
        y_ = lax.rem(y + d, n_y)
        block = w_block(k, y_ * 2 * slots, 2 * slots)
        return w_copy(block, base_p + d, partner)

    share = piece // n_y

    def wa_part(j, y_):
        return pl.ds(pl.multiple_of(j * piece + y_ * share, share), share)

    def wa_block(j):
        return wa.at[:, w_rows(j, 1)]

    def wa_scatter(d):
        y_ = lax.rem(y + d, n_y)
        src = w_attn.at[pl.ds(pl.multiple_of(y_ * share, share), share)]
        return remote(src, w_share.at[y], wa_send.at[d], wa_recv.at[y], y_peer[d - 1])

    def wa_keep():
        src = w_attn.at[pl.ds(pl.multiple_of(y * share, share), share)]
        return pltpu.make_async_copy(src, w_share.at[y], wa_recv.at[y])

    def wa_line(y_):
        return remote(
            w_share.at[y_],
            wa.at[t, wa_part(i, y)],
            wa_send.at[n_y + y_],
            wa_recv.at[n_y + t],
            2 * y_ + zh,
            "tp",
        )

    def wa_own(y_):
        return pltpu.make_async_copy(
            w_share.at[y_], wa.at[t, wa_part(i, y)], wa_recv.at[n_y + t]
        )

    def wa_flip():
        block = wa.at[:, wa_part(i, y)]
        return remote(block, block, wa_send.at[2 * n_y], wa_recv.at[n_y + n_tp], flip)

    def wa_up(d):
        block = wa.at[:, wa_part(i, y)]
        return remote(
            block, block, wa_send.at[2 * n_y + d], wa_recv.at[n_y + n_tp + d], y_peer[d - 1]
        )

    def wa_along(d):
        block = wa_block(i)
        return remote(
            block, block, wa_send.at[3 * n_y + d], wa_recv.at[2 * n_y + n_tp + d], x_peer[d - 1]
        )

    def wa_hand(d):
        block = wa_block(lax.rem(x + d, n_x) * 2 + k)
        n = n_x + d
        return remote(
            block, block, wa_send.at[3 * n_y + n], wa_recv.at[2 * n_y + n_tp + n], partner
        )

    def wa_landed(block, n):
        pltpu.make_async_copy(block, block, wa_recv.at[n]).wait()

    def wa_send_lines():
        for y_ in range(n_y):
            wa_landed(w_share.at[y_], y_)
        for y_ in range(n_y):

            @pl.when(2 * y_ + zh != t)
            def _():
                wa_line(y_).start()

            @pl.when(2 * y_ + zh == t)
            def _():
                wa_own(y_).start()

    def wa_collect():
        @pl.when(holder)
        def _():
            for s in range(n_tp):
                wa_landed(wa.at[s, wa_part(i, y)], n_y + s)
            wa_flip().start()
            for d in range(1, n_y):
                wa_up(d).start()

    def wa_spread():
        @pl.when(jnp.logical_not(holder))
        def _():
            wa_landed(wa.at[:, wa_part(i, y)], n_y + n_tp)
            for d in range(1, n_y):
                wa_up(d).start()

    def wa_rows_done():
        for d in range(1, n_y):
            wa_landed(wa.at[:, wa_part(i, lax.rem(y + n_y - d, n_y))], n_y + n_tp + d)
        for d in range(1, n_x):
            wa_along(d).start()
        wa_hand(0).start()

    def wa_hand_on():
        for d in range(1, n_x):
            j = lax.rem(x + n_x - d, n_x) * 2 + k
            wa_landed(wa_block(j), 2 * n_y + n_tp + d)
            wa_hand(n_x - d).start()

    def wa_done():
        for d in range(n_x):
            j = lax.rem(x + d, n_x) * 2 + 1 - k
            wa_landed(wa_block(j), 2 * n_y + n_tp + n_x + d)

    product = (hyena[0].astype(F32) * hyena[2].astype(F32)).astype(BF16)
    rim_out[...] = product[rows - taps :]

    def rim_copy():
        return remote(rim_out, rim, rim_send, rim_recv, after)

    w_flip().start()
    rim_copy().start()
    w_swap(w_hyena, me, 0).start()
    w_keep(w_hyena, me, 1).start()

    for d in range(1, n_y):
        wa_scatter(d).start()
    wa_keep().start()

    @pl.loop(0, heads)
    def _(h):
        flip_kv(h).start()
        start_own(h)

    w_landed(w_block(k, me, 1), 1)
    w_landed(w_block(k, partner, 1), 0)
    for d in range(1, n_x):
        w_along(d, 0).start()

    padded[pl.ds(taps, rows), :] = product.astype(F32)
    chunk = rows // 2

    def convolve(first):
        low = max(first - 8 * (taps // 8 - 1) + taps, 8)
        count = first + taps + chunk - low

        @pl.loop(0, width // 128)
        def _(tile):
            cols = pl.ds(pl.multiple_of(tile * 128, 128), 128)
            for s in range(8):
                shifted[s, pl.ds(low, count), :] = padded[pl.ds(low - s, count), cols]

            def eight(a, acc):
                coef = filters[pl.ds(pl.multiple_of(a * 8, 8), 8), cols]
                start = pl.multiple_of(taps + first - a * 8, 8)
                for s in range(8):
                    acc = acc + coef[s : s + 1, :] * shifted[s, pl.ds(start, chunk), :]
                return acc

            acc = lax.fori_loop(0, taps // 8, eight, jnp.zeros((chunk, 128), F32))
            gate = hyena[1, pl.ds(first, chunk), cols].astype(F32)
            act[pl.ds(first, chunk), cols] = (gate * acc).astype(BF16)

    if chunk >= taps:
        convolve(chunk)
    wa_send_lines()
    w_landed(w_far, 2)
    w_swap(w_far, flip, last).start()
    w_keep(w_far, flip, last + 1).start()
    w_landed(w_block(k, flip, 1), last + 1)
    w_landed(w_block(k, at(y, 1 - zh, x, 1 - k), 1), last)
    for d in range(1, n_x):
        w_along(d, 1).start()
    for d in range(1, n_x):
        x_ = lax.rem(x + n_x - d, n_x)
        w_landed(w_block(k, at(y, zh, x_, 0), 2), 2 + d)
    for d in range(1, n_x):
        x_ = lax.rem(x + n_x - d, n_x)
        w_landed(w_block(k, at(y, 1 - zh, x_, 0), 2), 2 + d + n_x - 1)
    for d in range(1, n_y):
        w_up(d).start()
    w_hand(0).start()
    spread(0)

    @pl.loop(0, heads // 2)
    def _(h):
        spread(h + 1)
        pass_on(h)

    for d in range(1, n_y):
        y_ = lax.rem(y + n_y - d, n_y)
        w_landed(w_block(k, y_ * 2 * slots, 2 * slots), base_y + d)
        w_hand(n_y - d).start()

    wa_collect()

    @pl.loop(heads // 2, heads)
    def _(h):
        @pl.when(h < heads - 1)
        def _():
            spread(h + 1)

        pass_on(h)

    def rs_copy(way, d, g):
        piece_of = (d, pl.ds(pl.multiple_of(g * half, half), half))
        buffer = (from_left, from_right)[way]
        return remote(
            part.at[piece_of],
            buffer.at[piece_of],
            rs_send.at[way, d, g],
            rs_recv.at[way, d, g],
            (t + 1, t - 1)[way],
            "tp",
        )

    def rs_add(way, d, g):
        piece_of = (d, pl.ds(pl.multiple_of(g * half, half), half))
        buffer = (from_left, from_right)[way]
        landed = buffer.at[piece_of]
        pltpu.make_async_copy(landed, landed, rs_recv.at[way, d, g]).wait()
        part[piece_of] = (part[piece_of].astype(F32) + buffer[piece_of].astype(F32)).astype(BF16)

    rs_steps = (n_tp - 1) * GROUPS

    def finish(out):
        total = part[t].astype(F32)
        for way in range(2):

            @pl.when((t > 0) if way == 0 else (t < n_tp - 1))
            def _():
                for g in range(GROUPS):
                    buffer = (from_left, from_right)[way]
                    landed = buffer.at[t, pl.ds(g * half, half)]
                    pltpu.make_async_copy(landed, landed, rs_recv.at[way, t, g]).wait()

        left = jnp.where(t > 0, from_left[t].astype(F32), 0.0)
        right = jnp.where(t < n_tp - 1, from_right[t].astype(F32), 0.0)
        out[...] = (total + left + right).astype(BF16)

    scale = 1.0 / math.sqrt(HEAD_DIM)
    gap = lax.broadcasted_iota(jnp.int32, (rows, rows), 1) - lax.broadcasted_iota(
        jnp.int32, (rows, rows), 0
    )

    def attend(h):
        queries = attn[0, :, lanes(h)]

        def block_scores(keys):
            return (
                lax.dot_general(
                    queries, keys, (((1,), (1,)), ((), ())), preferred_element_type=F32
                )
                * scale
            )

        def fold(op, block):
            kept = block[:, :128]
            for n in range(1, rows // 128):
                kept = op(kept, block[:, n * 128 : (n + 1) * 128])
            return kept

        own = jnp.where(gap <= 0, block_scores(attn[1, :, lanes(h)]), -jnp.inf)
        scores[:, slots * rows :] = own
        top = fold(jnp.maximum, own)
        for j in range(slots):
            least = jnp.where(i == j, 0, -rows)
            least = jnp.where((row == 0) & (i <= j), rows, least)
            block = jnp.where(gap > least, block_scores(kv[0, j, :, lanes(h)]), -jnp.inf)
            scores[:, j * rows : (j + 1) * rows] = block
            top = jnp.maximum(top, fold(jnp.maximum, block))
        top = jnp.max(top, axis=1, keepdims=True)
        total = jnp.zeros((rows, 128), F32)
        result = jnp.zeros((rows, HEAD_DIM), F32)
        for j in range(slots + 1):
            weights = jnp.exp(scores[:, j * rows : (j + 1) * rows] - top)
            total = total + fold(jnp.add, weights)
            values = attn[2, :, lanes(h)] if j == slots else kv[1, j, :, lanes(h)]
            result = result + jnp.dot(weights.astype(BF16), values, preferred_element_type=F32)
        total = jnp.sum(total, axis=1, keepdims=True)
        gathered[t, :, lanes(h)] = (result / total).astype(BF16)

    def ag_copy(h, way, s):
        block = gathered.at[s, :, lanes(h)]
        return remote(
            block, block, ag_send.at[h, way, s], ag_recv.at[h, s], (t + 1, t - 1)[way], "tp"
        )

    def ag_own(h):
        @pl.when(t < n_tp - 1)
        def _():
            ag_copy(h, 0, t).start()

        @pl.when(t > 0)
        def _():
            ag_copy(h, 1, t).start()

    def line_step(n):
        for g in range(GROUPS):
            for way in range(2):
                ahead = (t, n_tp - 1 - t)[way]
                more = ahead < n_tp - 1

                @pl.when(n <= ahead)
                def _():
                    s = (t - n, t + n)[way]
                    for h in range(g * heads // GROUPS, (g + 1) * heads // GROUPS):
                        block = gathered.at[s, :, lanes(h)]
                        pltpu.make_async_copy(block, block, ag_recv.at[h, s]).wait()

                        @pl.when(more)
                        def _():
                            ag_copy(h, way, s).start()

                @pl.when(n > ahead)
                def _():
                    m = n - ahead - 1
                    d = (n_tp - 1 - m, m)[way]

                    @pl.when(ahead > 0)
                    def _():
                        rs_add(way, d, g)

                    rs_copy(way, d, g).start()

    def add_source(s):
        scores[:, :dest_w] += lax.dot_general(
            gathered[s], wa[s], (((1,), (1,)), ((), ())), preferred_element_type=F32
        )

    def add_sources(hops):
        @pl.when(t >= hops)
        def _():
            add_source(t - hops)

        @pl.when(t + hops < n_tp)
        def _():
            add_source(t + hops)

    @pl.loop(0, heads)
    def _(h):
        rest(h)
        attend(h)
        ag_own(h)

    pltpu.make_async_copy(rim, rim, rim_recv).wait()
    padded[pl.ds(0, taps), :] = jnp.where(me > 0, rim[...].astype(F32), 0.0)
    convolve(0)
    if chunk < taps:
        convolve(chunk)

    for d in range(n_y):
        y_ = lax.rem(y + d, n_y)
        w_landed(w_block(1 - k, y_ * 2 * slots, 2 * slots), base_p + d)

    @pl.loop(0, n_tp)
    def _(d):
        weight = wg[pl.ds(pl.multiple_of(d * dest_w, dest_w), dest_w), :]
        part[d] = lax.dot_general(
            act[...], weight, (((1,), (1,)), ((), ())), preferred_element_type=F32
        ).astype(BF16)

    wa_spread()
    early = n_tp // 4 + 1
    late = n_tp - n_tp // 4

    @pl.loop(1, early)
    def _(n):
        line_step(n)

    wa_rows_done()

    @pl.loop(early, late)
    def _(n):
        line_step(n)

    wa_hand_on()
    wa_done()
    scores[:, :dest_w] = jnp.zeros((rows, dest_w), F32)
    add_source(t)

    @pl.loop(1, late)
    def _(n):
        add_sources(n)

    @pl.loop(late, n_tp)
    def _(n):
        line_step(n)
        add_sources(n)

    out_a[...] = scores[:, :dest_w].astype(BF16)
    finish(out_h)

    rim_copy().wait_send()
    w_swap(w_hyena, me, 0).wait_send()
    w_swap(w_far, flip, last).wait_send()
    w_flip().wait_send()
    for d in range(1, n_x):
        w_along(d, 0).wait_send()
        w_along(d, 1).wait_send()
    for d in range(1, n_y):
        w_up(d).wait_send()
    for d in range(n_y):
        w_hand(d).wait_send()

    @pl.loop(0, heads)
    def _(h):
        flip_kv(h).wait_send()
        for d in range(1, n_x):
            along(h, d, own_kv(h)).wait_send()
            forward(h, d).wait_send()
        to_partner(h, own_kv(h)).wait_send()

    @pl.loop(0, rs_steps)
    def _(step):
        m = step // GROUPS
        g = step % GROUPS

        @pl.when(t < n_tp - 1 - m)
        def _():
            rs_copy(0, n_tp - 1 - m, g).wait_send()

        @pl.when(t > m)
        def _():
            rs_copy(1, m, g).wait_send()

    for d in range(1, n_y):
        wa_scatter(d).wait_send()
        wa_up(d).wait_send()
    for y_ in range(n_y):

        @pl.when(2 * y_ + zh != t)
        def _():
            wa_line(y_).wait_send()

    @pl.when(holder)
    def _():
        wa_flip().wait_send()

    for d in range(1, n_x):
        wa_along(d).wait_send()
    for d in range(n_x):
        wa_hand(d).wait_send()

    @pl.loop(0, heads)
    def _(h):
        @pl.loop(0, n_tp)
        def _(s):
            @pl.when((s <= t) & (t < n_tp - 1))
            def _():
                ag_copy(h, 0, s).wait_send()

            @pl.when((s >= t) & (t > 0))
            def _():
                ag_copy(h, 1, s).wait_send()


def per_device(window, n_tp, hyena_in, filters, attn_in, out_weight, attn_weight):
    hyena = hyena_in.transpose(1, 0, 2)
    attn = attn_in.transpose(1, 0, 2)
    _, rows, width = attn.shape
    taps = filters.shape[0]
    piece = out_weight.shape[1]
    n_ctx = lax.axis_size("ctx")
    slots = window // rows
    n_x = slots // 2
    n_y = n_ctx // (2 * slots)
    columns = piece * n_ctx
    dest_w = columns // n_tp
    heads = width // HEAD_DIM
    n_w = 4 + 2 * n_x + 2 * n_y
    dma = pltpu.SemaphoreType.DMA
    result = jax.ShapeDtypeStruct((rows, dest_w), BF16)
    return pl.pallas_call(
        functools.partial(kernel, window),
        out_shape=(result, result),
        in_specs=[pl.BlockSpec(memory_space=pltpu.VMEM)] * 5,
        out_specs=(pl.BlockSpec(memory_space=pltpu.VMEM),) * 2,
        scratch_shapes=[
            pltpu.VMEM((2, slots, rows, width), BF16),
            pltpu.VMEM((columns, width), BF16),
            pltpu.VMEM((piece, width), BF16),
            pltpu.VMEM((n_y, piece // n_y, width), BF16),
            pltpu.VMEM((n_tp, dest_w, width), BF16),
            pltpu.VMEM((n_tp, rows, width), BF16),
            pltpu.VMEM((n_tp, rows, dest_w), BF16),
            pltpu.VMEM((n_tp, rows, dest_w), BF16),
            pltpu.VMEM((n_tp, rows, dest_w), BF16),
            pltpu.VMEM((taps, width), BF16),
            pltpu.VMEM((taps, width), BF16),
            pltpu.VMEM((taps + rows, width), F32),
            pltpu.VMEM((8, taps + rows, 128), F32),
            pltpu.VMEM((rows, width), BF16),
            pltpu.VMEM((rows, (slots + 1) * rows), F32),
            dma((heads, slots)),
            dma((heads, 2 * n_x)),
            dma((n_w,)),
            dma((n_w,)),
            dma((2, n_tp, GROUPS)),
            dma((2, n_tp, GROUPS)),
            dma,
            dma,
            dma((n_tp + 2 * n_y + 2 * n_x,)),
            dma((3 * n_y + 2 * n_x,)),
            dma((heads, n_tp)),
            dma((heads, 2, n_tp)),
        ],
        compiler_params=pltpu.CompilerParams(
            collective_id=0, has_side_effects=True, vmem_limit_bytes=60 * 2**20
        ),
    )(hyena, filters, attn, out_weight.T, attn_weight.T)


def build(mesh, window):
    in_specs = (
        P("ctx", None, "tp"),
        P(None, "tp"),
        P("ctx", None, "tp"),
        P("tp", "ctx"),
        P("tp", "ctx"),
    )
    return jax.shard_map(
        functools.partial(per_device, window, mesh.shape["tp"]),
        mesh=mesh,
        in_specs=in_specs,
        out_specs=(P("ctx", "tp"), P("ctx", "tp")),
        check_vma=False,
    )


def solution(mesh):
    return build(mesh, WINDOW)
```

```python
import functools
import math

import jax
import jax.numpy as jnp
from jax import lax
from jax.experimental import pallas as pl
from jax.experimental.pallas import tpu as pltpu
from jax.sharding import PartitionSpec as P

HEAD_DIM = 128
WINDOW = 2048
GROUPS = 2
F32 = jnp.float32
BF16 = jnp.bfloat16


def kernel(
    window,
    hyena,
    filters,
    attn,
    w_hyena,
    w_attn,
    out_h,
    out_a,
    kv,
    wg,
    w_far,
    w_share,
    wa,
    gathered,
    part,
    from_left,
    from_right,
    rim_out,
    rim,
    padded,
    shifted,
    act,
    scores,
    kv_recv,
    kv_send,
    w_recv,
    w_send,
    rs_recv,
    rs_send,
    rim_recv,
    rim_send,
    wa_recv,
    wa_send,
    ag_recv,
    ag_send,
):
    _, rows, width = attn.shape
    heads = width // HEAD_DIM
    taps = filters.shape[0]
    n_ctx = lax.axis_size("ctx")
    n_tp = lax.axis_size("tp")
    slots = window // rows
    n_x = slots // 2
    n_y = n_ctx // (2 * slots)
    piece = w_hyena.shape[0]
    pair = 2 * piece
    row_w = slots * piece
    dest_w = out_h.shape[1]
    half = rows // GROUPS

    me = lax.axis_index("ctx")
    t = lax.axis_index("tp")
    row = me // slots
    i = me % slots
    y = row // 2
    zh = row % 2
    x = i // 2
    k = i % 2
    n_rows = n_ctx // slots

    def at(y_, zh_, x_, k_):
        return ((y_ * 2 + zh_) * n_x + x_) * 2 + k_

    partner = at(y, zh, x, 1 - k)
    flip = at(y, 1 - zh, x, k)
    row_next = lax.rem(row + 1, n_rows) * slots + i
    row_prev = lax.rem(row + n_rows - 1, n_rows) * slots + i
    after = lax.rem(me + 1, n_ctx)
    before = lax.rem(me + n_ctx - 1, n_ctx)
    x_peer = [at(y, zh, lax.rem(x + d, n_x), k) for d in range(1, n_x)]
    y_peer = [at(lax.rem(y + d, n_y), zh, x, k) for d in range(1, n_y)]

    barrier = pltpu.get_barrier_semaphore()
    peers = [partner, flip, row_next, row_prev, after, before] + x_peer + y_peer
    for peer in peers:
        pl.semaphore_signal(barrier, inc=1, device_id={"ctx": peer})

    @pl.when(t > 0)
    def _():
        pl.semaphore_signal(barrier, inc=1, device_id={"tp": t - 1})

    @pl.when(t < n_tp - 1)
    def _():
        pl.semaphore_signal(barrier, inc=1, device_id={"tp": t + 1})

    beside = (t > 0).astype(jnp.int32) + (t < n_tp - 1).astype(jnp.int32)

    holder = t % 2 == zh

    @pl.when(holder)
    def _():
        for s in range(n_tp):

            @pl.when(s != t)
            def _():
                pl.semaphore_signal(barrier, inc=1, device_id={"tp": s})

    collectors = n_tp // 2 - holder.astype(jnp.int32)
    pl.semaphore_wait(barrier, len(peers) + beside + collectors)

    def remote(src, dst, send, recv, peer, axis="ctx"):
        return pltpu.make_async_remote_copy(
            src_ref=src, dst_ref=dst, send_sem=send, recv_sem=recv, device_id={axis: peer}
        )

    def lanes(h):
        return pl.ds(pl.multiple_of(h * HEAD_DIM, HEAD_DIM), HEAD_DIM)

    def own_kv(h):
        return attn.at[pl.ds(1, 2), :, lanes(h)]

    def slot_kv(j, h):
        return kv.at[:, j, :, lanes(h)]

    def kv_copy(src, h, j, n, peer):
        return remote(src, slot_kv(j, h), kv_send.at[h, n], kv_recv.at[h, j], peer)

    def flip_kv(h):
        return kv_copy(own_kv(h), h, i, 0, row_next)

    def along(h, d, src):
        return kv_copy(src, h, i, d, x_peer[d - 1])

    def to_partner(h, src):
        return kv_copy(src, h, i, n_x, partner)

    def came(d):
        return lax.rem(x + d, n_x) * 2 + k

    def forward(h, d):
        j = came(d)
        return kv_copy(slot_kv(j, h), h, j, n_x + d, partner)

    def start_own(h):
        for d in range(1, n_x):

            @pl.when(x + d < n_x)
            def _():
                along(h, d, own_kv(h)).start()

        @pl.when(k == 0)
        def _():
            to_partner(h, own_kv(h)).start()

    def arrived(h, j):
        pltpu.make_async_copy(slot_kv(j, h), slot_kv(j, h), kv_recv.at[h, j]).wait()

    def spread(h):
        arrived(h, i)
        for d in range(1, n_x):

            @pl.when(x + d >= n_x)
            def _():
                along(h, d, slot_kv(i, h)).start()

        @pl.when(k == 1)
        def _():
            to_partner(h, slot_kv(i, h)).start()

    def pass_on(h):
        for d in range(1, n_x):
            arrived(h, came(d))
            forward(h, d).start()

    def rest(h):
        for d in range(n_x):
            arrived(h, lax.rem(x + d, n_x) * 2 + 1 - k)

    side_w = width // 2

    def side(k_):
        return pl.ds(pl.multiple_of(k_ * side_w, side_w), side_w)

    def w_rows(first, count):
        return pl.ds(pl.multiple_of(first * piece, piece), count * piece)

    def w_block(k_, first, count):
        return wg.at[w_rows(first, count), side(k_)]

    def w_copy(block, n, peer):
        return remote(block, block, w_send.at[n], w_recv.at[n], peer)

    def w_swap(src, owner, n):
        return remote(
            src.at[:, side(1 - k)], w_block(1 - k, owner, 1), w_send.at[n], w_recv.at[n], partner
        )

    def w_keep(src, owner, n):
        return pltpu.make_async_copy(src.at[:, side(k)], w_block(k, owner, 1), w_recv.at[n])

    def w_landed(block, n):
        pltpu.make_async_copy(block, block, w_recv.at[n]).wait()

    chip = me - k
    chip_flip = flip - k

    last = 2 + 2 * n_x + 2 * n_y

    def w_flip():
        return remote(w_hyena, w_far, w_send.at[2], w_recv.at[2], flip)

    def w_along(d, other):
        return w_copy(
            w_block(k, chip_flip if other else chip, 2), 2 + d + (n_x - 1) * other, x_peer[d - 1]
        )

    base_y = 2 + 2 * n_x - 1

    def w_up(d):
        return w_copy(w_block(k, y * 2 * slots, 2 * slots), base_y + d, y_peer[d - 1])

    base_p = base_y + n_y

    def w_hand(d):
        y_ = lax.rem(y + d, n_y)
        block = w_block(k, y_ * 2 * slots, 2 * slots)
        return w_copy(block, base_p + d, partner)

    share = piece // n_y

    def wa_part(j, y_):
        return pl.ds(pl.multiple_of(j * piece + y_ * share, share), share)

    def wa_block(j):
        return wa.at[:, w_rows(j, 1)]

    def wa_scatter(d):
        y_ = lax.rem(y + d, n_y)
        src = w_attn.at[pl.ds(pl.multiple_of(y_ * share, share), share)]
        return remote(src, w_share.at[y], wa_send.at[d], wa_recv.at[y], y_peer[d - 1])

    def wa_keep():
        src = w_attn.at[pl.ds(pl.multiple_of(y * share, share), share)]
        return pltpu.make_async_copy(src, w_share.at[y], wa_recv.at[y])

    def wa_line(y_):
        return remote(
            w_share.at[y_],
            wa.at[t, wa_part(i, y)],
            wa_send.at[n_y + y_],
            wa_recv.at[n_y + t],
            2 * y_ + zh,
            "tp",
        )

    def wa_own(y_):
        return pltpu.make_async_copy(
            w_share.at[y_], wa.at[t, wa_part(i, y)], wa_recv.at[n_y + t]
        )

    def wa_flip():
        block = wa.at[:, wa_part(i, y)]
        return remote(block, block, wa_send.at[2 * n_y], wa_recv.at[n_y + n_tp], flip)

    def wa_up(d):
        block = wa.at[:, wa_part(i, y)]
        return remote(
            block, block, wa_send.at[2 * n_y + d], wa_recv.at[n_y + n_tp + d], y_peer[d - 1]
        )

    def wa_along(d):
        block = wa_block(i)
        return remote(
            block, block, wa_send.at[3 * n_y + d], wa_recv.at[2 * n_y + n_tp + d], x_peer[d - 1]
        )

    def wa_hand(d):
        block = wa_block(lax.rem(x + d, n_x) * 2 + k)
        n = n_x + d
        return remote(
            block, block, wa_send.at[3 * n_y + n], wa_recv.at[2 * n_y + n_tp + n], partner
        )

    def wa_landed(block, n):
        pltpu.make_async_copy(block, block, wa_recv.at[n]).wait()

    def wa_send_lines():
        for y_ in range(n_y):
            wa_landed(w_share.at[y_], y_)
        for y_ in range(n_y):

            @pl.when(2 * y_ + zh != t)
            def _():
                wa_line(y_).start()

            @pl.when(2 * y_ + zh == t)
            def _():
                wa_own(y_).start()

    def wa_collect():
        @pl.when(holder)
        def _():
            for s in range(n_tp):
                wa_landed(wa.at[s, wa_part(i, y)], n_y + s)
            wa_flip().start()
            for d in range(1, n_y):
                wa_up(d).start()

    def wa_spread():
        @pl.when(jnp.logical_not(holder))
        def _():
            wa_landed(wa.at[:, wa_part(i, y)], n_y + n_tp)
            for d in range(1, n_y):
                wa_up(d).start()

    def wa_rows_done():
        for d in range(1, n_y):
            wa_landed(wa.at[:, wa_part(i, lax.rem(y + n_y - d, n_y))], n_y + n_tp + d)
        for d in range(1, n_x):
            wa_along(d).start()
        wa_hand(0).start()

    def wa_hand_on():
        for d in range(1, n_x):
            j = lax.rem(x + n_x - d, n_x) * 2 + k
            wa_landed(wa_block(j), 2 * n_y + n_tp + d)
            wa_hand(n_x - d).start()

    def wa_done():
        for d in range(n_x):
            j = lax.rem(x + d, n_x) * 2 + 1 - k
            wa_landed(wa_block(j), 2 * n_y + n_tp + n_x + d)

    product = (hyena[0].astype(F32) * hyena[2].astype(F32)).astype(BF16)
    rim_out[...] = product[rows - taps :]

    def rim_copy():
        return remote(rim_out, rim, rim_send, rim_recv, after)

    w_flip().start()
    rim_copy().start()
    w_swap(w_hyena, me, 0).start()
    w_keep(w_hyena, me, 1).start()

    for d in range(1, n_y):
        wa_scatter(d).start()
    wa_keep().start()

    @pl.loop(0, heads)
    def _(h):
        flip_kv(h).start()
        start_own(h)

    w_landed(w_block(k, me, 1), 1)
    w_landed(w_block(k, partner, 1), 0)
    for d in range(1, n_x):
        w_along(d, 0).start()

    padded[pl.ds(taps, rows), :] = product.astype(F32)
    chunk = rows // 2

    def convolve(first):
        low = max(first - 8 * (taps // 8 - 1) + taps, 8)
        count = first + taps + chunk - low

        @pl.loop(0, width // 128)
        def _(tile):
            cols = pl.ds(pl.multiple_of(tile * 128, 128), 128)
            for s in range(8):
                shifted[s, pl.ds(low, count), :] = padded[pl.ds(low - s, count), cols]

            def eight(a, acc):
                coef = filters[pl.ds(pl.multiple_of(a * 8, 8), 8), cols]
                start = pl.multiple_of(taps + first - a * 8, 8)
                for s in range(8):
                    acc = acc + coef[s : s + 1, :] * shifted[s, pl.ds(start, chunk), :]
                return acc

            acc = lax.fori_loop(0, taps // 8, eight, jnp.zeros((chunk, 128), F32))
            gate = hyena[1, pl.ds(first, chunk), cols].astype(F32)
            act[pl.ds(first, chunk), cols] = (gate * acc).astype(BF16)

    if chunk >= taps:
        convolve(chunk)
    wa_send_lines()
    w_landed(w_far, 2)
    w_swap(w_far, flip, last).start()
    w_keep(w_far, flip, last + 1).start()
    w_landed(w_block(k, flip, 1), last + 1)
    w_landed(w_block(k, at(y, 1 - zh, x, 1 - k), 1), last)
    for d in range(1, n_x):
        w_along(d, 1).start()
    for d in range(1, n_x):
        x_ = lax.rem(x + n_x - d, n_x)
        w_landed(w_block(k, at(y, zh, x_, 0), 2), 2 + d)
    for d in range(1, n_x):
        x_ = lax.rem(x + n_x - d, n_x)
        w_landed(w_block(k, at(y, 1 - zh, x_, 0), 2), 2 + d + n_x - 1)
    for d in range(1, n_y):
        w_up(d).start()
    w_hand(0).start()
    def rs_copy(way, d, g):
        piece_of = (d, pl.ds(pl.multiple_of(g * half, half), half))
        buffer = (from_left, from_right)[way]
        return remote(
            part.at[piece_of],
            buffer.at[piece_of],
            rs_send.at[way, d, g],
            rs_recv.at[way, d, g],
            (t + 1, t - 1)[way],
            "tp",
        )

    def rs_add(way, d, g):
        piece_of = (d, pl.ds(pl.multiple_of(g * half, half), half))
        buffer = (from_left, from_right)[way]
        landed = buffer.at[piece_of]
        pltpu.make_async_copy(landed, landed, rs_recv.at[way, d, g]).wait()
        part[piece_of] = (part[piece_of].astype(F32) + buffer[piece_of].astype(F32)).astype(BF16)

    rs_steps = (n_tp - 1) * GROUPS

    def finish(out):
        total = part[t].astype(F32)
        for way in range(2):

            @pl.when((t > 0) if way == 0 else (t < n_tp - 1))
            def _():
                for g in range(GROUPS):
                    buffer = (from_left, from_right)[way]
                    landed = buffer.at[t, pl.ds(g * half, half)]
                    pltpu.make_async_copy(landed, landed, rs_recv.at[way, t, g]).wait()

        left = jnp.where(t > 0, from_left[t].astype(F32), 0.0)
        right = jnp.where(t < n_tp - 1, from_right[t].astype(F32), 0.0)
        out[...] = (total + left + right).astype(BF16)

    scale = 1.0 / math.sqrt(HEAD_DIM)
    gap = lax.broadcasted_iota(jnp.int32, (rows, rows), 1) - lax.broadcasted_iota(
        jnp.int32, (rows, rows), 0
    )

    def attend(h):
        queries = attn[0, :, lanes(h)]

        def block_scores(keys):
            return (
                lax.dot_general(
                    queries, keys, (((1,), (1,)), ((), ())), preferred_element_type=F32
                )
                * scale
            )

        def fold(op, block):
            kept = block[:, :128]
            for n in range(1, rows // 128):
                kept = op(kept, block[:, n * 128 : (n + 1) * 128])
            return kept

        own = jnp.where(gap <= 0, block_scores(attn[1, :, lanes(h)]), -jnp.inf)
        scores[:, slots * rows :] = own
        top = fold(jnp.maximum, own)
        for j in range(slots):
            least = jnp.where(i == j, 0, -rows)
            least = jnp.where((row == 0) & (i <= j), rows, least)
            block = jnp.where(gap > least, block_scores(kv[0, j, :, lanes(h)]), -jnp.inf)
            scores[:, j * rows : (j + 1) * rows] = block
            top = jnp.maximum(top, fold(jnp.maximum, block))
        top = jnp.max(top, axis=1, keepdims=True)
        total = jnp.zeros((rows, 128), F32)
        result = jnp.zeros((rows, HEAD_DIM), F32)
        for j in range(slots + 1):
            weights = jnp.exp(scores[:, j * rows : (j + 1) * rows] - top)
            total = total + fold(jnp.add, weights)
            values = attn[2, :, lanes(h)] if j == slots else kv[1, j, :, lanes(h)]
            result = result + jnp.dot(weights.astype(BF16), values, preferred_element_type=F32)
        total = jnp.sum(total, axis=1, keepdims=True)
        gathered[t, :, lanes(h)] = (result / total).astype(BF16)

    def ag_copy(h, way, s):
        block = gathered.at[s, :, lanes(h)]
        return remote(
            block, block, ag_send.at[h, way, s], ag_recv.at[h, s], (t + 1, t - 1)[way], "tp"
        )

    def ag_own(h):
        @pl.when(t < n_tp - 1)
        def _():
            ag_copy(h, 0, t).start()

        @pl.when(t > 0)
        def _():
            ag_copy(h, 1, t).start()

    def line_step(n):
        for g in range(GROUPS):
            for way in range(2):
                ahead = (t, n_tp - 1 - t)[way]
                more = ahead < n_tp - 1

                @pl.when(n <= ahead)
                def _():
                    s = (t - n, t + n)[way]
                    for h in range(g * heads // GROUPS, (g + 1) * heads // GROUPS):
                        block = gathered.at[s, :, lanes(h)]
                        pltpu.make_async_copy(block, block, ag_recv.at[h, s]).wait()

                        @pl.when(more)
                        def _():
                            ag_copy(h, way, s).start()

                @pl.when(n > ahead)
                def _():
                    m = n - ahead - 1
                    d = (n_tp - 1 - m, m)[way]

                    @pl.when(ahead > 0)
                    def _():
                        rs_add(way, d, g)

                    rs_copy(way, d, g).start()

    def add_source(s):
        scores[:, :dest_w] += lax.dot_general(
            gathered[s], wa[s], (((1,), (1,)), ((), ())), preferred_element_type=F32
        )

    def add_sources(hops):
        @pl.when(t >= hops)
        def _():
            add_source(t - hops)

        @pl.when(t + hops < n_tp)
        def _():
            add_source(t + hops)

    def turn(h):
        rest(h)
        attend(h)
        ag_own(h)

    spread(0)

    @pl.loop(0, heads // 2)
    def _(h):
        spread(h + 1)
        pass_on(h)

        @pl.when(h > 0)
        def _():
            turn(h - 1)

    for d in range(1, n_y):
        y_ = lax.rem(y + n_y - d, n_y)
        w_landed(w_block(k, y_ * 2 * slots, 2 * slots), base_y + d)
        w_hand(n_y - d).start()

    wa_collect()
    pltpu.make_async_copy(rim, rim, rim_recv).wait()
    padded[pl.ds(0, taps), :] = jnp.where(me > 0, rim[...].astype(F32), 0.0)
    convolve(0)
    if chunk < taps:
        convolve(chunk)

    @pl.loop(heads // 2, heads)
    def _(h):
        @pl.when(h < heads - 1)
        def _():
            spread(h + 1)

        pass_on(h)
        turn(h - 1)

    turn(heads - 1)
    for d in range(n_y):
        y_ = lax.rem(y + d, n_y)
        w_landed(w_block(1 - k, y_ * 2 * slots, 2 * slots), base_p + d)

    @pl.loop(0, n_tp)
    def _(d):
        weight = wg[pl.ds(pl.multiple_of(d * dest_w, dest_w), dest_w), :]
        part[d] = lax.dot_general(
            act[...], weight, (((1,), (1,)), ((), ())), preferred_element_type=F32
        ).astype(BF16)

    wa_spread()
    late = n_tp - 1

    line_step(1)
    wa_rows_done()

    @pl.loop(2, late - 1)
    def _(n):
        line_step(n)

    wa_hand_on()

    @pl.loop(max(late - 1, 2), late)
    def _(n):
        line_step(n)

    wa_done()
    scores[:, :dest_w] = jnp.zeros((rows, dest_w), F32)
    add_source(t)

    @pl.loop(1, late)
    def _(n):
        add_sources(n)

    @pl.loop(max(late, 2), n_tp)
    def _(n):
        line_step(n)

    @pl.loop(late, n_tp)
    def _(n):
        add_sources(n)

    out_a[...] = scores[:, :dest_w].astype(BF16)
    finish(out_h)

    rim_copy().wait_send()
    w_swap(w_hyena, me, 0).wait_send()
    w_swap(w_far, flip, last).wait_send()
    w_flip().wait_send()
    for d in range(1, n_x):
        w_along(d, 0).wait_send()
        w_along(d, 1).wait_send()
    for d in range(1, n_y):
        w_up(d).wait_send()
    for d in range(n_y):
        w_hand(d).wait_send()

    @pl.loop(0, heads)
    def _(h):
        flip_kv(h).wait_send()
        for d in range(1, n_x):
            along(h, d, own_kv(h)).wait_send()
            forward(h, d).wait_send()
        to_partner(h, own_kv(h)).wait_send()

    @pl.loop(0, rs_steps)
    def _(step):
        m = step // GROUPS
        g = step % GROUPS

        @pl.when(t < n_tp - 1 - m)
        def _():
            rs_copy(0, n_tp - 1 - m, g).wait_send()

        @pl.when(t > m)
        def _():
            rs_copy(1, m, g).wait_send()

    for d in range(1, n_y):
        wa_scatter(d).wait_send()
        wa_up(d).wait_send()
    for y_ in range(n_y):

        @pl.when(2 * y_ + zh != t)
        def _():
            wa_line(y_).wait_send()

    @pl.when(holder)
    def _():
        wa_flip().wait_send()

    for d in range(1, n_x):
        wa_along(d).wait_send()
    for d in range(n_x):
        wa_hand(d).wait_send()

    @pl.loop(0, heads)
    def _(h):
        @pl.loop(0, n_tp)
        def _(s):
            @pl.when((s <= t) & (t < n_tp - 1))
            def _():
                ag_copy(h, 0, s).wait_send()

            @pl.when((s >= t) & (t > 0))
            def _():
                ag_copy(h, 1, s).wait_send()


def per_device(window, n_tp, hyena_in, filters, attn_in, out_weight, attn_weight):
    hyena = hyena_in.transpose(1, 0, 2)
    attn = attn_in.transpose(1, 0, 2)
    _, rows, width = attn.shape
    taps = filters.shape[0]
    piece = out_weight.shape[1]
    n_ctx = lax.axis_size("ctx")
    slots = window // rows
    n_x = slots // 2
    n_y = n_ctx // (2 * slots)
    columns = piece * n_ctx
    dest_w = columns // n_tp
    heads = width // HEAD_DIM
    n_w = 4 + 2 * n_x + 2 * n_y
    dma = pltpu.SemaphoreType.DMA
    result = jax.ShapeDtypeStruct((rows, dest_w), BF16)
    return pl.pallas_call(
        functools.partial(kernel, window),
        out_shape=(result, result),
        in_specs=[pl.BlockSpec(memory_space=pltpu.VMEM)] * 5,
        out_specs=(pl.BlockSpec(memory_space=pltpu.VMEM),) * 2,
        scratch_shapes=[
            pltpu.VMEM((2, slots, rows, width), BF16),
            pltpu.VMEM((columns, width), BF16),
            pltpu.VMEM((piece, width), BF16),
            pltpu.VMEM((n_y, piece // n_y, width), BF16),
            pltpu.VMEM((n_tp, dest_w, width), BF16),
            pltpu.VMEM((n_tp, rows, width), BF16),
            pltpu.VMEM((n_tp, rows, dest_w), BF16),
            pltpu.VMEM((n_tp, rows, dest_w), BF16),
            pltpu.VMEM((n_tp, rows, dest_w), BF16),
            pltpu.VMEM((taps, width), BF16),
            pltpu.VMEM((taps, width), BF16),
            pltpu.VMEM((taps + rows, width), F32),
            pltpu.VMEM((8, taps + rows, 128), F32),
            pltpu.VMEM((rows, width), BF16),
            pltpu.VMEM((rows, (slots + 1) * rows), F32),
            dma((heads, slots)),
            dma((heads, 2 * n_x)),
            dma((n_w,)),
            dma((n_w,)),
            dma((2, n_tp, GROUPS)),
            dma((2, n_tp, GROUPS)),
            dma,
            dma,
            dma((n_tp + 2 * n_y + 2 * n_x,)),
            dma((3 * n_y + 2 * n_x,)),
            dma((heads, n_tp)),
            dma((heads, 2, n_tp)),
        ],
        compiler_params=pltpu.CompilerParams(
            collective_id=0, has_side_effects=True, vmem_limit_bytes=60 * 2**20
        ),
    )(hyena, filters, attn, out_weight.T, attn_weight.T)


def build(mesh, window):
    in_specs = (
        P("ctx", None, "tp"),
        P(None, "tp"),
        P("ctx", None, "tp"),
        P("tp", "ctx"),
        P("tp", "ctx"),
    )
    return jax.shard_map(
        functools.partial(per_device, window, mesh.shape["tp"]),
        mesh=mesh,
        in_specs=in_specs,
        out_specs=(P("ctx", "tp"), P("ctx", "tp")),
        check_vma=False,
    )


def solution(mesh):
    return build(mesh, WINDOW)
```

```python
import functools
import math

import jax
import jax.numpy as jnp
from jax import lax
from jax.experimental import pallas as pl
from jax.experimental.pallas import tpu as pltpu
from jax.sharding import PartitionSpec as P

HEAD_DIM = 128
WINDOW = 2048
GROUPS = 2
F32 = jnp.float32
BF16 = jnp.bfloat16


def kernel(
    window,
    hyena,
    filters,
    attn,
    w_hyena,
    w_attn,
    out_h,
    out_a,
    kv,
    wg,
    w_far,
    w_share,
    wa,
    gathered,
    part,
    from_left,
    from_right,
    rim_out,
    rim,
    padded,
    shifted,
    act,
    scores,
    kv_recv,
    kv_send,
    w_recv,
    w_send,
    rs_recv,
    rs_send,
    rim_recv,
    rim_send,
    wa_recv,
    wa_send,
    ag_recv,
    ag_send,
):
    _, rows, width = attn.shape
    heads = width // HEAD_DIM
    taps = filters.shape[0]
    n_ctx = lax.axis_size("ctx")
    n_tp = lax.axis_size("tp")
    slots = window // rows
    n_x = slots // 2
    n_y = n_ctx // (2 * slots)
    piece = w_hyena.shape[0]
    pair = 2 * piece
    row_w = slots * piece
    dest_w = out_h.shape[1]
    half = rows // GROUPS

    me = lax.axis_index("ctx")
    t = lax.axis_index("tp")
    row = me // slots
    i = me % slots
    y = row // 2
    zh = row % 2
    x = i // 2
    k = i % 2
    n_rows = n_ctx // slots

    def at(y_, zh_, x_, k_):
        return ((y_ * 2 + zh_) * n_x + x_) * 2 + k_

    partner = at(y, zh, x, 1 - k)
    flip = at(y, 1 - zh, x, k)
    row_next = lax.rem(row + 1, n_rows) * slots + i
    row_prev = lax.rem(row + n_rows - 1, n_rows) * slots + i
    after = lax.rem(me + 1, n_ctx)
    before = lax.rem(me + n_ctx - 1, n_ctx)
    x_peer = [at(y, zh, lax.rem(x + d, n_x), k) for d in range(1, n_x)]
    y_peer = [at(lax.rem(y + d, n_y), zh, x, k) for d in range(1, n_y)]

    barrier = pltpu.get_barrier_semaphore()
    peers = [partner, flip, row_next, row_prev, after, before] + x_peer + y_peer
    for peer in peers:
        pl.semaphore_signal(barrier, inc=1, device_id={"ctx": peer})

    @pl.when(t > 0)
    def _():
        pl.semaphore_signal(barrier, inc=1, device_id={"tp": t - 1})

    @pl.when(t < n_tp - 1)
    def _():
        pl.semaphore_signal(barrier, inc=1, device_id={"tp": t + 1})

    beside = (t > 0).astype(jnp.int32) + (t < n_tp - 1).astype(jnp.int32)

    holder = t % 2 == zh

    @pl.when(holder)
    def _():
        for s in range(n_tp):

            @pl.when(s != t)
            def _():
                pl.semaphore_signal(barrier, inc=1, device_id={"tp": s})

    collectors = n_tp // 2 - holder.astype(jnp.int32)
    pl.semaphore_wait(barrier, len(peers) + beside + collectors)

    def remote(src, dst, send, recv, peer, axis="ctx"):
        return pltpu.make_async_remote_copy(
            src_ref=src, dst_ref=dst, send_sem=send, recv_sem=recv, device_id={axis: peer}
        )

    def lanes(h):
        return pl.ds(pl.multiple_of(h * HEAD_DIM, HEAD_DIM), HEAD_DIM)

    def own_kv(h):
        return attn.at[pl.ds(1, 2), :, lanes(h)]

    def slot_kv(j, h):
        return kv.at[:, j, :, lanes(h)]

    def kv_copy(src, h, j, n, peer):
        return remote(src, slot_kv(j, h), kv_send.at[h, n], kv_recv.at[h, j], peer)

    def flip_kv(h):
        return kv_copy(own_kv(h), h, i, 0, row_next)

    def along(h, d, src):
        return kv_copy(src, h, i, d, x_peer[d - 1])

    def to_partner(h, src):
        return kv_copy(src, h, i, n_x, partner)

    def came(d):
        return lax.rem(x + d, n_x) * 2 + k

    def forward(h, d):
        j = came(d)
        return kv_copy(slot_kv(j, h), h, j, n_x + d, partner)

    def start_own(h):
        for d in range(1, n_x):

            @pl.when(x + d < n_x)
            def _():
                along(h, d, own_kv(h)).start()

        @pl.when(k == 0)
        def _():
            to_partner(h, own_kv(h)).start()

    def arrived(h, j):
        pltpu.make_async_copy(slot_kv(j, h), slot_kv(j, h), kv_recv.at[h, j]).wait()

    def spread(h):
        arrived(h, i)
        for d in range(1, n_x):

            @pl.when(x + d >= n_x)
            def _():
                along(h, d, slot_kv(i, h)).start()

        @pl.when(k == 1)
        def _():
            to_partner(h, slot_kv(i, h)).start()

    def pass_on(h):
        for d in range(1, n_x):
            arrived(h, came(d))
            forward(h, d).start()

    def rest(h):
        for d in range(n_x):
            arrived(h, lax.rem(x + d, n_x) * 2 + 1 - k)

    side_w = width // 2

    def side(k_):
        return pl.ds(pl.multiple_of(k_ * side_w, side_w), side_w)

    def w_rows(first, count):
        return pl.ds(pl.multiple_of(first * piece, piece), count * piece)

    def w_block(k_, first, count):
        return wg.at[w_rows(first, count), side(k_)]

    def w_copy(block, n, peer):
        return remote(block, block, w_send.at[n], w_recv.at[n], peer)

    def w_swap(src, owner, n):
        return remote(
            src.at[:, side(1 - k)], w_block(1 - k, owner, 1), w_send.at[n], w_recv.at[n], partner
        )

    def w_keep(src, owner, n):
        return pltpu.make_async_copy(src.at[:, side(k)], w_block(k, owner, 1), w_recv.at[n])

    def w_landed(block, n):
        pltpu.make_async_copy(block, block, w_recv.at[n]).wait()

    chip = me - k
    chip_flip = flip - k

    last = 2 + 2 * n_x + 2 * n_y

    def w_flip():
        return remote(w_hyena, w_far, w_send.at[2], w_recv.at[2], flip)

    def w_along(d, other):
        return w_copy(
            w_block(k, chip_flip if other else chip, 2), 2 + d + (n_x - 1) * other, x_peer[d - 1]
        )

    base_y = 2 + 2 * n_x - 1

    def w_up(d):
        return w_copy(w_block(k, y * 2 * slots, 2 * slots), base_y + d, y_peer[d - 1])

    base_p = base_y + n_y

    def w_hand(d):
        y_ = lax.rem(y + d, n_y)
        block = w_block(k, y_ * 2 * slots, 2 * slots)
        return w_copy(block, base_p + d, partner)

    share = piece // n_y

    def wa_part(j, y_):
        return pl.ds(pl.multiple_of(j * piece + y_ * share, share), share)

    def wa_block(j):
        return wa.at[:, w_rows(j, 1)]

    def wa_scatter(d):
        y_ = lax.rem(y + d, n_y)
        src = w_attn.at[pl.ds(pl.multiple_of(y_ * share, share), share)]
        return remote(src, w_share.at[y], wa_send.at[d], wa_recv.at[y], y_peer[d - 1])

    def wa_keep():
        src = w_attn.at[pl.ds(pl.multiple_of(y * share, share), share)]
        return pltpu.make_async_copy(src, w_share.at[y], wa_recv.at[y])

    def wa_line(y_):
        return remote(
            w_share.at[y_],
            wa.at[t, wa_part(i, y)],
            wa_send.at[n_y + y_],
            wa_recv.at[n_y + t],
            2 * y_ + zh,
            "tp",
        )

    def wa_own(y_):
        return pltpu.make_async_copy(
            w_share.at[y_], wa.at[t, wa_part(i, y)], wa_recv.at[n_y + t]
        )

    def wa_flip():
        block = wa.at[:, wa_part(i, y)]
        return remote(block, block, wa_send.at[2 * n_y], wa_recv.at[n_y + n_tp], flip)

    def wa_up(d):
        block = wa.at[:, wa_part(i, y)]
        return remote(
            block, block, wa_send.at[2 * n_y + d], wa_recv.at[n_y + n_tp + d], y_peer[d - 1]
        )

    def wa_along(d):
        block = wa_block(i)
        return remote(
            block, block, wa_send.at[3 * n_y + d], wa_recv.at[2 * n_y + n_tp + d], x_peer[d - 1]
        )

    def wa_hand(d):
        block = wa_block(lax.rem(x + d, n_x) * 2 + k)
        n = n_x + d
        return remote(
            block, block, wa_send.at[3 * n_y + n], wa_recv.at[2 * n_y + n_tp + n], partner
        )

    def wa_landed(block, n):
        pltpu.make_async_copy(block, block, wa_recv.at[n]).wait()

    def wa_send_lines():
        for y_ in range(n_y):
            wa_landed(w_share.at[y_], y_)
        for y_ in range(n_y):

            @pl.when(2 * y_ + zh != t)
            def _():
                wa_line(y_).start()

            @pl.when(2 * y_ + zh == t)
            def _():
                wa_own(y_).start()

    def wa_collect():
        @pl.when(holder)
        def _():
            for s in range(n_tp):
                wa_landed(wa.at[s, wa_part(i, y)], n_y + s)
            wa_flip().start()
            for d in range(1, n_y):
                wa_up(d).start()

    def wa_spread():
        @pl.when(jnp.logical_not(holder))
        def _():
            wa_landed(wa.at[:, wa_part(i, y)], n_y + n_tp)
            for d in range(1, n_y):
                wa_up(d).start()

    def wa_rows_done():
        for d in range(1, n_y):
            wa_landed(wa.at[:, wa_part(i, lax.rem(y + n_y - d, n_y))], n_y + n_tp + d)
        for d in range(1, n_x):
            wa_along(d).start()
        wa_hand(0).start()

    def wa_hand_on():
        for d in range(1, n_x):
            j = lax.rem(x + n_x - d, n_x) * 2 + k
            wa_landed(wa_block(j), 2 * n_y + n_tp + d)
            wa_hand(n_x - d).start()

    def wa_done():
        for d in range(n_x):
            j = lax.rem(x + d, n_x) * 2 + 1 - k
            wa_landed(wa_block(j), 2 * n_y + n_tp + n_x + d)

    product = (hyena[0].astype(F32) * hyena[2].astype(F32)).astype(BF16)
    rim_out[...] = product[rows - taps :]

    def rim_copy():
        return remote(rim_out, rim, rim_send, rim_recv, after)

    w_flip().start()
    rim_copy().start()
    w_swap(w_hyena, me, 0).start()
    w_keep(w_hyena, me, 1).start()

    for d in range(1, n_y):
        wa_scatter(d).start()
    wa_keep().start()

    @pl.loop(0, heads)
    def _(h):
        flip_kv(h).start()
        start_own(h)

    w_landed(w_block(k, me, 1), 1)
    w_landed(w_block(k, partner, 1), 0)
    for d in range(1, n_x):
        w_along(d, 0).start()

    padded[pl.ds(taps, rows), :] = product.astype(F32)
    chunk = rows // 2

    def convolve(first):
        low = max(first - 8 * (taps // 8 - 1) + taps, 8)
        count = first + taps + chunk - low

        @pl.loop(0, width // 128)
        def _(tile):
            cols = pl.ds(pl.multiple_of(tile * 128, 128), 128)
            for s in range(8):
                shifted[s, pl.ds(low, count), :] = padded[pl.ds(low - s, count), cols]

            def eight(a, acc):
                coef = filters[pl.ds(pl.multiple_of(a * 8, 8), 8), cols]
                start = pl.multiple_of(taps + first - a * 8, 8)
                for s in range(8):
                    acc = acc + coef[s : s + 1, :] * shifted[s, pl.ds(start, chunk), :]
                return acc

            acc = lax.fori_loop(0, taps // 8, eight, jnp.zeros((chunk, 128), F32))
            gate = hyena[1, pl.ds(first, chunk), cols].astype(F32)
            act[pl.ds(first, chunk), cols] = (gate * acc).astype(BF16)

    if chunk >= taps:
        convolve(chunk)
    wa_send_lines()
    w_landed(w_far, 2)
    w_swap(w_far, flip, last).start()
    w_keep(w_far, flip, last + 1).start()
    w_landed(w_block(k, flip, 1), last + 1)
    w_landed(w_block(k, at(y, 1 - zh, x, 1 - k), 1), last)
    for d in range(1, n_x):
        w_along(d, 1).start()
    for d in range(1, n_x):
        x_ = lax.rem(x + n_x - d, n_x)
        w_landed(w_block(k, at(y, zh, x_, 0), 2), 2 + d)
    for d in range(1, n_x):
        x_ = lax.rem(x + n_x - d, n_x)
        w_landed(w_block(k, at(y, 1 - zh, x_, 0), 2), 2 + d + n_x - 1)
    for d in range(1, n_y):
        w_up(d).start()
    w_hand(0).start()
    def rs_copy(way, d, g):
        piece_of = (d, pl.ds(pl.multiple_of(g * half, half), half))
        buffer = (from_left, from_right)[way]
        return remote(
            part.at[piece_of],
            buffer.at[piece_of],
            rs_send.at[way, d, g],
            rs_recv.at[way, d, g],
            (t + 1, t - 1)[way],
            "tp",
        )

    def rs_add(way, d, g):
        piece_of = (d, pl.ds(pl.multiple_of(g * half, half), half))
        buffer = (from_left, from_right)[way]
        landed = buffer.at[piece_of]
        pltpu.make_async_copy(landed, landed, rs_recv.at[way, d, g]).wait()
        part[piece_of] = (part[piece_of].astype(F32) + buffer[piece_of].astype(F32)).astype(BF16)

    rs_steps = (n_tp - 1) * GROUPS

    def finish(out):
        total = part[t].astype(F32)
        for way in range(2):

            @pl.when((t > 0) if way == 0 else (t < n_tp - 1))
            def _():
                for g in range(GROUPS):
                    buffer = (from_left, from_right)[way]
                    landed = buffer.at[t, pl.ds(g * half, half)]
                    pltpu.make_async_copy(landed, landed, rs_recv.at[way, t, g]).wait()

        left = jnp.where(t > 0, from_left[t].astype(F32), 0.0)
        right = jnp.where(t < n_tp - 1, from_right[t].astype(F32), 0.0)
        out[...] = (total + left + right).astype(BF16)

    scale = 1.0 / math.sqrt(HEAD_DIM)
    gap = lax.broadcasted_iota(jnp.int32, (rows, rows), 1) - lax.broadcasted_iota(
        jnp.int32, (rows, rows), 0
    )

    def attend(h):
        queries = attn[0, :, lanes(h)]

        def block_scores(keys):
            return (
                lax.dot_general(
                    queries, keys, (((1,), (1,)), ((), ())), preferred_element_type=F32
                )
                * scale
            )

        def fold(op, block):
            kept = block[:, :128]
            for n in range(1, rows // 128):
                kept = op(kept, block[:, n * 128 : (n + 1) * 128])
            return kept

        own = jnp.where(gap <= 0, block_scores(attn[1, :, lanes(h)]), -jnp.inf)
        scores[:, slots * rows :] = own
        top = fold(jnp.maximum, own)
        for j in range(slots):
            least = jnp.where(i == j, 0, -rows)
            least = jnp.where((row == 0) & (i <= j), rows, least)
            block = jnp.where(gap > least, block_scores(kv[0, j, :, lanes(h)]), -jnp.inf)
            scores[:, j * rows : (j + 1) * rows] = block
            top = jnp.maximum(top, fold(jnp.maximum, block))
        top = jnp.max(top, axis=1, keepdims=True)
        total = jnp.zeros((rows, 128), F32)
        result = jnp.zeros((rows, HEAD_DIM), F32)
        for j in range(slots + 1):
            weights = jnp.exp(scores[:, j * rows : (j + 1) * rows] - top)
            total = total + fold(jnp.add, weights)
            values = attn[2, :, lanes(h)] if j == slots else kv[1, j, :, lanes(h)]
            result = result + jnp.dot(weights.astype(BF16), values, preferred_element_type=F32)
        total = jnp.sum(total, axis=1, keepdims=True)
        gathered[t, :, lanes(h)] = (result / total).astype(BF16)

    def ag_copy(h, way, s):
        block = gathered.at[s, :, lanes(h)]
        return remote(
            block, block, ag_send.at[h, way, s], ag_recv.at[h, s], (t + 1, t - 1)[way], "tp"
        )

    def ag_own(h):
        @pl.when(t < n_tp - 1)
        def _():
            ag_copy(h, 0, t).start()

        @pl.when(t > 0)
        def _():
            ag_copy(h, 1, t).start()

    def line_step(n):
        for g in range(GROUPS):
            for way in range(2):
                ahead = (t, n_tp - 1 - t)[way]
                more = ahead < n_tp - 1

                @pl.when(n <= ahead)
                def _():
                    s = (t - n, t + n)[way]
                    for h in range(g * heads // GROUPS, (g + 1) * heads // GROUPS):
                        block = gathered.at[s, :, lanes(h)]
                        pltpu.make_async_copy(block, block, ag_recv.at[h, s]).wait()

                        @pl.when(more)
                        def _():
                            ag_copy(h, way, s).start()

                @pl.when(n > ahead)
                def _():
                    m = n - ahead - 1
                    d = (n_tp - 1 - m, m)[way]

                    @pl.when(ahead > 0)
                    def _():
                        rs_add(way, d, g)

                    rs_copy(way, d, g).start()

    def add_source(s):
        scores[:, :dest_w] += lax.dot_general(
            gathered[s], wa[s], (((1,), (1,)), ((), ())), preferred_element_type=F32
        )

    def add_sources(hops):
        @pl.when(t >= hops)
        def _():
            add_source(t - hops)

        @pl.when(t + hops < n_tp)
        def _():
            add_source(t + hops)

    def turn(h):
        rest(h)
        attend(h)
        ag_own(h)

    spread(0)

    @pl.loop(0, heads // 2)
    def _(h):
        spread(h + 1)
        pass_on(h)

        @pl.when(h > 0)
        def _():
            turn(h - 1)

    for d in range(1, n_y):
        y_ = lax.rem(y + n_y - d, n_y)
        w_landed(w_block(k, y_ * 2 * slots, 2 * slots), base_y + d)
        w_hand(n_y - d).start()

    wa_collect()
    pltpu.make_async_copy(rim, rim, rim_recv).wait()
    padded[pl.ds(0, taps), :] = jnp.where(me > 0, rim[...].astype(F32), 0.0)
    convolve(0)
    if chunk < taps:
        convolve(chunk)

    @pl.loop(heads // 2, heads)
    def _(h):
        @pl.when(h < heads - 1)
        def _():
            spread(h + 1)

        pass_on(h)
        turn(h - 1)

    turn(heads - 1)
    for d in range(n_y):
        y_ = lax.rem(y + d, n_y)
        w_landed(w_block(1 - k, y_ * 2 * slots, 2 * slots), base_p + d)

    @pl.loop(0, n_tp)
    def _(d):
        weight = wg[pl.ds(pl.multiple_of(d * dest_w, dest_w), dest_w), :]
        part[d] = lax.dot_general(
            act[...], weight, (((1,), (1,)), ((), ())), preferred_element_type=F32
        ).astype(BF16)

    wa_spread()
    late = n_tp - 1

    line_step(1)
    wa_rows_done()

    rim_copy().wait_send()
    w_swap(w_hyena, me, 0).wait_send()
    w_swap(w_far, flip, last).wait_send()
    w_flip().wait_send()
    for d in range(1, n_x):
        w_along(d, 0).wait_send()
        w_along(d, 1).wait_send()
    for d in range(1, n_y):
        w_up(d).wait_send()
    for d in range(n_y):
        w_hand(d).wait_send()

    @pl.loop(0, heads)
    def _(h):
        flip_kv(h).wait_send()
        for d in range(1, n_x):
            along(h, d, own_kv(h)).wait_send()
            forward(h, d).wait_send()
        to_partner(h, own_kv(h)).wait_send()

    @pl.loop(2, late - 1)
    def _(n):
        line_step(n)

    wa_hand_on()

    @pl.loop(max(late - 1, 2), late)
    def _(n):
        line_step(n)

    wa_done()
    scores[:, :dest_w] = jnp.zeros((rows, dest_w), F32)
    add_source(t)

    @pl.loop(1, late)
    def _(n):
        add_sources(n)

    @pl.loop(max(late, 2), n_tp)
    def _(n):
        line_step(n)

    @pl.loop(late, n_tp)
    def _(n):
        add_sources(n)

    for d in range(1, n_y):
        wa_scatter(d).wait_send()
        wa_up(d).wait_send()
    for y_ in range(n_y):

        @pl.when(2 * y_ + zh != t)
        def _():
            wa_line(y_).wait_send()

    @pl.when(holder)
    def _():
        wa_flip().wait_send()

    for d in range(1, n_x):
        wa_along(d).wait_send()
    for d in range(n_x):
        wa_hand(d).wait_send()

    @pl.loop(0, heads)
    def _(h):
        @pl.loop(0, n_tp)
        def _(s):
            @pl.when((s <= t) & (t < n_tp - 1))
            def _():
                ag_copy(h, 0, s).wait_send()

            @pl.when((s >= t) & (t > 0))
            def _():
                ag_copy(h, 1, s).wait_send()

    out_a[...] = scores[:, :dest_w].astype(BF16)
    finish(out_h)

    @pl.loop(0, rs_steps)
    def _(step):
        m = step // GROUPS
        g = step % GROUPS

        @pl.when(t < n_tp - 1 - m)
        def _():
            rs_copy(0, n_tp - 1 - m, g).wait_send()

        @pl.when(t > m)
        def _():
            rs_copy(1, m, g).wait_send()


def per_device(window, n_tp, hyena_in, filters, attn_in, out_weight, attn_weight):
    hyena = hyena_in.transpose(1, 0, 2)
    attn = attn_in.transpose(1, 0, 2)
    _, rows, width = attn.shape
    taps = filters.shape[0]
    piece = out_weight.shape[1]
    n_ctx = lax.axis_size("ctx")
    slots = window // rows
    n_x = slots // 2
    n_y = n_ctx // (2 * slots)
    columns = piece * n_ctx
    dest_w = columns // n_tp
    heads = width // HEAD_DIM
    n_w = 4 + 2 * n_x + 2 * n_y
    dma = pltpu.SemaphoreType.DMA
    result = jax.ShapeDtypeStruct((rows, dest_w), BF16)
    return pl.pallas_call(
        functools.partial(kernel, window),
        out_shape=(result, result),
        in_specs=[pl.BlockSpec(memory_space=pltpu.VMEM)] * 5,
        out_specs=(pl.BlockSpec(memory_space=pltpu.VMEM),) * 2,
        scratch_shapes=[
            pltpu.VMEM((2, slots, rows, width), BF16),
            pltpu.VMEM((columns, width), BF16),
            pltpu.VMEM((piece, width), BF16),
            pltpu.VMEM((n_y, piece // n_y, width), BF16),
            pltpu.VMEM((n_tp, dest_w, width), BF16),
            pltpu.VMEM((n_tp, rows, width), BF16),
            pltpu.VMEM((n_tp, rows, dest_w), BF16),
            pltpu.VMEM((n_tp, rows, dest_w), BF16),
            pltpu.VMEM((n_tp, rows, dest_w), BF16),
            pltpu.VMEM((taps, width), BF16),
            pltpu.VMEM((taps, width), BF16),
            pltpu.VMEM((taps + rows, width), F32),
            pltpu.VMEM((8, taps + rows, 128), F32),
            pltpu.VMEM((rows, width), BF16),
            pltpu.VMEM((rows, (slots + 1) * rows), F32),
            dma((heads, slots)),
            dma((heads, 2 * n_x)),
            dma((n_w,)),
            dma((n_w,)),
            dma((2, n_tp, GROUPS)),
            dma((2, n_tp, GROUPS)),
            dma,
            dma,
            dma((n_tp + 2 * n_y + 2 * n_x,)),
            dma((3 * n_y + 2 * n_x,)),
            dma((heads, n_tp)),
            dma((heads, 2, n_tp)),
        ],
        compiler_params=pltpu.CompilerParams(
            collective_id=0, has_side_effects=True, vmem_limit_bytes=60 * 2**20
        ),
    )(hyena, filters, attn, out_weight.T, attn_weight.T)


def build(mesh, window):
    in_specs = (
        P("ctx", None, "tp"),
        P(None, "tp"),
        P("ctx", None, "tp"),
        P("tp", "ctx"),
        P("tp", "ctx"),
    )
    return jax.shard_map(
        functools.partial(per_device, window, mesh.shape["tp"]),
        mesh=mesh,
        in_specs=in_specs,
        out_specs=(P("ctx", "tp"), P("ctx", "tp")),
        check_vma=False,
    )


def solution(mesh):
    return build(mesh, WINDOW)
```
